512 devices in a mesh: region: 32 (over x, z), tm: 16 (over y, core).
Axes of the slice: x: 4, y: 8, z: 8, core: 2. Of those that a mesh axis runs over, the one named last changes fastest.
Arguments:
- right_side: float32 [1024, 65536], P('tm', 'region'), may hold values from -9 to 9
- initial: float32 [1024, 65536], P('tm', 'region'), may hold values from -1.5 to 1.5
- blocks: bfloat16 [512, 9, 128, 128], P(('region', 'tm')), may hold values from -2.5 to 3.1, as said below
- neighbour_blocks: int32 [512, 8], P('region'), may hold values from 0 to 511, as said below
- temporal_cov: bfloat16 [1024, 1024], P('tm'), may hold values from -2.5 to 2.8, as said below
Outputs:
- solution: float32 [1024, 65536], P('tm', 'region')
- residual: float32 [1024, 65536], P('tm', 'region')
The draws below stay inside these ranges and needn't reach their ends.
Inputs may be any that keep to these rules, and one draw needn't show every extreme that they name: blocks[i, 0] is symmetric positive definite. `neighbour_blocks`: each column names every block exactly once. Blocks fall into cyclic windows of 16 consecutive blocks starting at 8 + m * 16, and every block listed for row i lies in the window of i. temporal_cov is symmetric positive definite.
All inputs are finite; a program needn't handle non-finite values.
Results may differ from the reference program's by a relative error of at most 0.012.
The reference program's roundings to bfloat16 on the way count: a program that leaves them out, or rounds other values in their place, can miss the bound.
Values may be sent and summed in bfloat16 or wider, within the bound.
No kernel may reach another device: no remote copies, remote signals or barrier semaphores. Data moves between devices by JAX's collectives and lax.ppermute only.
A program may use at most 64 MiB of HBM per device.

```python
import jax
import jax.numpy as jnp
from jax import lax

HOURS = 1024
BLK = 128
NBR = 9
ITERS = 2
ROWS_REGION = 16
BLOCKS = 512
SITES = 65536
N_REGION = 32


def draw_right_side(key, part):
    hour_place = (jnp.arange(HOURS, dtype=jnp.float32) / HOURS)[:, None]
    site_place = (jnp.arange(SITES, dtype=jnp.float32) / SITES)[None, :]
    scale_ramp = jnp.sqrt((1.0 + 2.0 * hour_place) * (1.0 + 2.0 * site_place))
    noise_base = jnp.clip(jax.random.normal(key, (HOURS, SITES), jnp.float32), -3.0, 3.0)
    return noise_base * scale_ramp


def draw_blocks(key, part):
    key_diag = jax.random.fold_in(key, 11)
    key_off = jax.random.fold_in(key, 12)
    key_sing = jax.random.fold_in(key, 13)
    raw_diag = jnp.clip(jax.random.normal(key_diag, (BLOCKS, BLK, BLK), jnp.float32), -3.0, 3.0)
    lowest = 0.05
    diagonal = 0.25 * jnp.einsum('nab,ncb->nac', raw_diag, raw_diag, precision=lax.Precision.HIGHEST) / BLK
    diagonal = diagonal + 0.8 * jnp.eye(BLK, dtype=jnp.float32)[None]
    mixing = jax.random.normal(key_off, (BLOCKS, NBR - 1, BLK, BLK), jnp.float32)
    orthogonal, upper_part = jnp.linalg.qr(mixing)
    singular = jax.random.uniform(key_sing, (BLOCKS, NBR - 1, 1, BLK), jnp.float32, lowest, 0.1)
    coupling = orthogonal * singular
    whole = jnp.concatenate([diagonal[:, None], coupling], axis=1)
    return whole.astype(jnp.bfloat16)


def draw_neighbour_blocks(key, part):
    regions = BLOCKS // ROWS_REGION
    half_rows = ROWS_REGION // 2
    block_ids = jnp.arange(BLOCKS, dtype=jnp.int32)
    shifted = jnp.mod(block_ids - half_rows, BLOCKS)
    window = shifted // ROWS_REGION
    within = shifted % ROWS_REGION
    columns = []
    for column in range(NBR - 1):
        window_keys = jax.random.split(jax.random.fold_in(key, 101 + column), regions)
        orders = jax.vmap(lambda one_key: jax.random.permutation(one_key, ROWS_REGION))(window_keys)
        landed = window * ROWS_REGION + orders[window, within].astype(jnp.int32)
        columns.append(jnp.mod(landed + half_rows, BLOCKS))
    return jnp.stack(columns, axis=1).astype(jnp.int32)


def draw_temporal_cov(key, part):
    raw_hours = jnp.clip(jax.random.normal(key, (HOURS, HOURS), jnp.float32), -3.0, 3.0)
    gram = jnp.dot(raw_hours, raw_hours.T, precision=lax.Precision.HIGHEST)
    covariance = 0.25 * gram / HOURS + 0.5 * jnp.eye(HOURS, dtype=jnp.float32)
    return covariance.astype(jnp.bfloat16)


def steps_of(stream_key, shape, pieces, least, top_value):
    def one(position, parts):
        draws = jax.random.uniform(jax.random.fold_in(jax.random.fold_in(stream_key, 6), position), (parts,), jnp.float32, least / len(pieces), top_value / len(pieces))
        return jnp.repeat(jnp.exp(draws), shape[position] // parts).reshape((-1,) + (1,) * (len(shape) - position - 1))

    gain = one(*pieces[0])
    for cut in pieces[1:]:
        gain = gain * one(*cut)
    return gain


def bell_draw(key, dims, spread, limit, cuts=(), kind=jnp.bfloat16):
    values = jax.random.normal(key, dims, jnp.float32) * spread
    if len(cuts) > 0:
        values = steps_of(key, dims, cuts, -0.22, 0.18) * values
    return jnp.clip(values, min=-limit, max=limit).astype(kind)


def setup_inputs(seed: int = 0) -> dict:
    key_list = jax.random.split(jax.random.key(seed), 6)
    right_side = draw_right_side(jax.random.fold_in(key_list[5], 71), 0)
    initial = bell_draw(key_list[1], (HOURS, SITES), 0.25, 1.5, ((0, 16), (1, 32)), jnp.float32)
    blocks = draw_blocks(jax.random.fold_in(key_list[5], 71), 0)
    neighbour_blocks = draw_neighbour_blocks(jax.random.fold_in(key_list[5], 71), 0)
    temporal_cov = draw_temporal_cov(jax.random.fold_in(key_list[5], 71), 0)
    return {"right_side": right_side, "initial": initial, "blocks": blocks, "neighbour_blocks": neighbour_blocks, "temporal_cov": temporal_cov}


def spatial_product(lowered, blocks, neighbour_blocks):
    cell_tiles = lowered.astype(jnp.float32).reshape(HOURS, BLOCKS, BLK)
    itself = jnp.arange(BLOCKS, dtype=jnp.int32)[:, None]
    places = jnp.concatenate([itself, neighbour_blocks.astype(jnp.int32)], axis=1)
    places = places.reshape(N_REGION, ROWS_REGION, NBR)
    grouped = blocks.reshape(N_REGION, ROWS_REGION, NBR, BLK, BLK)

    def one_region(paired):
        region_places, region_blocks = paired
        gathered = jnp.take(cell_tiles, region_places, axis=1)
        return jnp.einsum('hrkb,rkab->hra', gathered, region_blocks.astype(jnp.float32), precision=lax.Precision.HIGHEST)
    per_region = lax.map(one_region, (places, grouped))
    return jnp.transpose(per_region, (1, 0, 2, 3)).reshape(HOURS, SITES)

def operate(current, blocks, neighbour_blocks, temporal_cov):
    lowered = current.astype(jnp.bfloat16)
    spatial = spatial_product(lowered, blocks, neighbour_blocks).astype(jnp.bfloat16)
    blended = jnp.dot(temporal_cov.astype(jnp.float32), spatial.astype(jnp.float32), precision=lax.Precision.HIGHEST)
    return current + blended.astype(jnp.bfloat16).astype(jnp.float32)

def reference(right_side, initial, blocks, neighbour_blocks, temporal_cov):
    solution = initial
    residual = right_side - operate(initial, blocks, neighbour_blocks, temporal_cov)
    direction = residual
    norm_now = jnp.sum(residual * residual)
    for iteration in range(ITERS):
        applied = operate(direction, blocks, neighbour_blocks, temporal_cov)
        step_size = norm_now / jnp.sum(direction * applied)
        solution = solution + step_size * direction
        residual = residual - step_size * applied
        norm_next = jnp.sum(residual * residual)
        direction = residual + norm_next / norm_now * direction
        norm_now = norm_next
    return (solution, residual)
```

```python
import jax
import jax.numpy as jnp
from jax import lax
from jax.experimental import pallas as pl
from jax.experimental.pallas import tpu as pltpu
from jax.sharding import Mesh
from jax.sharding import PartitionSpec as P

REGION = ("region_0", "region_1")
TM = ("tm_0", "tm_1")
REGION_TM = ("region_0", "region_1", "tm_0", "tm_1")
F32 = jnp.float32
BF16 = jnp.bfloat16
VMEM = pl.BlockSpec(memory_space=pltpu.MemorySpace.VMEM)
SMEM = pl.BlockSpec(memory_space=pltpu.MemorySpace.SMEM)


def dot(a, b):
    return jnp.dot(a, b, preferred_element_type=F32)


def temporal_kernel(c_ref, v_ref, w_ref, shift_ref):
    hours, wide = v_ref.shape
    n = wide // 2
    row = lax.broadcasted_iota(jnp.int32, (n, n), 0)
    col = lax.broadcasted_iota(jnp.int32, (n, n), 1)
    diagonal = jnp.zeros((n, n), F32)
    for k in range(hours // n):
        tile = c_ref[k * n : (k + 1) * n, k * n : (k + 1) * n].astype(F32)
        diagonal = diagonal + jnp.where(row == col, tile, 0.0)
    c0 = jnp.sum(diagonal, axis=(0, 1), keepdims=True) / hours
    shift_ref[...] = jnp.broadcast_to(c0, shift_ref.shape)
    v = v_ref[...]
    first = (dot(c_ref[...], v) - c0 * v.astype(F32)).astype(BF16)
    w_ref[:, :wide] = first
    second = (dot(c_ref[...], first) - c0 * first.astype(F32)).astype(BF16)
    w_ref[:, wide : 2 * wide] = second
    third = second[:, :n]
    w_ref[:, 2 * wide :] = (dot(c_ref[...], third) - c0 * third.astype(F32)).astype(BF16)


def spatial_kernel(
    slots_ref, g_ref, xd_ref, shift_ref, b_ref, low_ref, high_ref, gram_ref, b_buf, f_buf, z_buf, w_buf, sums, sem
):
    rows, hours, n = f_buf.shape[0], xd_ref.shape[1], xd_ref.shape[2] // 2
    half = rows // 2
    slots = slots_ref.shape[1]

    def load(i):
        return pltpu.make_async_copy(b_ref.at[i], b_buf.at[i], sem.at[i])

    for i in range(rows):
        load(i).start()
    c0 = shift_ref[0:1, 0:1]
    for i in range(rows):
        x = xd_ref[i, :, 0:n].astype(F32)
        y1 = g_ref[i, :, 0:n].astype(F32)
        y2 = g_ref[i, :, 2 * n : 3 * n].astype(F32)
        y3 = g_ref[i, :, 4 * n : 5 * n].astype(F32)
        f_buf[i, 0:hours, :] = (c0 * x + y1).astype(BF16)
        f_buf[i, hours : 2 * hours, :] = (c0 * y1 + y2).astype(BF16)
        f_buf[i, 2 * hours :, :] = (c0 * y2 + y3).astype(BF16)

    def product(source, i):
        tiles = [source[i]] + [source[slots_ref[i, k]] for k in range(slots)]
        return dot(jnp.concatenate(tiles, axis=1), b_buf[i])

    def split(value):
        top = value.astype(BF16)
        return top, (value - top.astype(F32)).astype(BF16)

    def put(k, i, value):
        @pl.when(i < half)
        def _():
            low_ref[k, i] = value

        @pl.when(i >= half)
        def _():
            high_ref[k, i - half] = value

    def get(k, i):
        return jnp.where(i < half, low_ref[k, jnp.minimum(i, half - 1)], high_ref[k, jnp.maximum(i - half, 0)])

    def stage_one(i, _):
        load(i).wait()
        out = product(f_buf, i)
        d = xd_ref[i, :, n : 2 * n].astype(F32)
        e1 = g_ref[i, :, n : 2 * n].astype(F32)
        e2 = g_ref[i, :, 3 * n : 4 * n].astype(F32)
        r0 = d - out[0:hours]
        u1 = e1 - out[hours : 2 * hours]
        u2 = e2 - out[2 * hours :]
        put(0, i, r0)
        for k, z in enumerate((c0 * r0 + u1, c0 * (c0 * r0 + 2.0 * u1) + u2)):
            top, rest = split(z)
            z_buf[i, 2 * k * hours : (2 * k + 1) * hours, :] = top
            z_buf[i, (2 * k + 1) * hours : (2 * k + 2) * hours, :] = rest
        return 0

    def stage_two(i, _):
        out = product(z_buf, i)
        put(1, i, out[0:hours] + out[hours : 2 * hours])
        top, rest = split(out[2 * hours : 3 * hours] + out[3 * hours :])
        w_buf[i, 0:hours, :] = top
        w_buf[i, hours:, :] = rest
        return 0

    def add(k, value):
        sums[k] += jnp.sum(value.reshape(hours // 8, 8, n), axis=0)

    def stage_three(i, _):
        out = product(w_buf, i)
        m2 = out[0:hours] + out[hours:]
        put(2, i, m2)
        r0, m1 = get(0, i), get(1, i)
        add(0, r0 * r0)
        add(1, r0 * m1)
        add(2, m1 * m1)
        add(3, r0 * m2)
        add(4, m1 * m2)
        return 0

    sums[...] = jnp.zeros_like(sums)
    lax.fori_loop(0, rows, stage_one, 0)
    lax.fori_loop(0, rows, stage_two, 0)
    lax.fori_loop(0, rows, stage_three, 0)
    gram = jnp.sum(sums[...], axis=1)
    for k in range(gram_ref.shape[0]):
        gram_ref[k] = gram


def finish_kernel(gram_ref, x_ref, low_ref, high_ref, solution_ref, residual_ref):
    total = jnp.sum(jnp.sum(gram_ref[...], axis=0), axis=1, keepdims=True)
    rr, rm1, m11, rm2, m12 = (total[k : k + 1, 0:1] for k in range(5))
    rq = rr + rm1
    qq = rr + 2.0 * rm1 + m11
    rs = rr + 2.0 * rm1 + rm2
    qs = rr + 3.0 * rm1 + rm2 + 2.0 * m11 + m12
    alpha = rr / rq
    norm = rr - 2.0 * alpha * rq + alpha * alpha * qq
    keep = 1.0 + norm / rr
    curvature = keep * keep * rq - alpha * keep * (rs + qq) + alpha * alpha * qs
    step = norm / curvature
    half, n = low_ref.shape[1], low_ref.shape[3]
    for part, ref in ((0, low_ref), (1, high_ref)):
        for i in range(half):
            lanes = slice((part * half + i) * n, (part * half + i + 1) * n)
            r0, m1, m2 = ref[0, i], ref[1, i], ref[2, i]
            q = r0 + m1
            p1 = keep * r0 - alpha * q
            image = keep * q - alpha * (q + m1 + m2)
            solution_ref[:, lanes] = x_ref[:, lanes] + alpha * r0 + step * p1
            residual_ref[:, lanes] = r0 - alpha * q - step * image


def local(right_side, initial, blocks, neighbour_blocks, temporal_cov):
    hours, sites = right_side.shape
    n = blocks.shape[2]
    width = blocks.shape[1]
    rows = neighbour_blocks.shape[0]
    half = rows // 2
    slots = neighbour_blocks.shape[1]
    tm_count = lax.axis_size(TM)
    regions = lax.axis_size(REGION)

    covariance = lax.all_gather(temporal_cov, TM, axis=0, tiled=True)

    x = initial.astype(BF16).reshape(hours, rows, 1, n)
    d = (right_side - initial).astype(BF16).reshape(hours, rows, 1, n)
    pack = jnp.concatenate([x, d], axis=2).transpose(1, 0, 2, 3).reshape(rows, hours, 2 * n)
    local_slots = jnp.mod(neighbour_blocks, rows)
    extra = jnp.pad(local_slots[:half].astype(BF16)[:, None, :], ((0, 0), (0, 15), (0, 2 * n - slots)))
    shifted = lax.ppermute(
        jnp.concatenate([pack[:half], extra], axis=1), REGION, [((r + 1) % regions, r) for r in range(regions)]
    )
    xd = jnp.concatenate([shifted[:, :hours], pack[half:]], axis=0)
    window_slots = jnp.concatenate([shifted[:, hours, :slots].astype(jnp.int32), local_slots[half:]], axis=0)

    pairs = [
        (((r + (t < half)) % regions) * tm_count + t, r * tm_count + t) for r in range(regions) for t in range(tm_count)
    ]
    flipped = jnp.swapaxes(blocks[0], 1, 2).reshape(1, width * n, n)
    window_blocks = lax.all_gather(lax.ppermute(flipped, REGION_TM, pairs), TM, axis=0, tiled=True)

    arrived = lax.all_to_all(xd, TM, split_axis=0, concat_axis=0, tiled=True)
    powers, shift = pl.pallas_call(
        temporal_kernel,
        out_shape=(
            jax.ShapeDtypeStruct((tm_count * hours, 5 * n), BF16),
            jax.ShapeDtypeStruct((8, n), F32),
        ),
        in_specs=[VMEM, VMEM],
        out_specs=(VMEM, VMEM),
        name="temporal",
    )(covariance, arrived.reshape(tm_count * hours, 2 * n))
    returned = lax.all_to_all(powers.reshape(tm_count, hours, 5 * n), TM, split_axis=0, concat_axis=0, tiled=True)

    low, high, gram = pl.pallas_call(
        spatial_kernel,
        out_shape=(
            jax.ShapeDtypeStruct((3, half, hours, n), F32),
            jax.ShapeDtypeStruct((3, half, hours, n), F32),
            jax.ShapeDtypeStruct((tm_count, 8, n), F32),
        ),
        in_specs=[SMEM, VMEM, VMEM, VMEM, pl.BlockSpec(memory_space=pl.ANY)],
        out_specs=(VMEM, VMEM, VMEM),
        scratch_shapes=[
            pltpu.VMEM((rows, width * n, n), BF16),
            pltpu.VMEM((rows, 3 * hours, n), BF16),
            pltpu.VMEM((rows, 4 * hours, n), BF16),
            pltpu.VMEM((rows, 2 * hours, n), BF16),
            pltpu.VMEM((8, 8, n), F32),
            pltpu.SemaphoreType.DMA((rows,)),
        ],
        name="spatial",
    )(window_slots, returned, xd, shift, window_blocks)

    back = lax.ppermute(low, REGION, [(r, (r + 1) % regions) for r in range(regions)])
    over_tm = lax.all_to_all(gram, TM, split_axis=0, concat_axis=0, tiled=True)
    spread = jnp.broadcast_to(jnp.sum(over_tm, axis=0)[None], (regions, 8, n))
    over_region = lax.all_to_all(spread, REGION, split_axis=0, concat_axis=0, tiled=True)
    return pl.pallas_call(
        finish_kernel,
        out_shape=(
            jax.ShapeDtypeStruct((hours, sites), F32),
            jax.ShapeDtypeStruct((hours, sites), F32),
        ),
        in_specs=[VMEM, VMEM, VMEM, VMEM],
        out_specs=(VMEM, VMEM),
        name="finish",
    )(over_region, initial, back, high)


def solution(mesh):
    split = Mesh(mesh.devices.reshape(4, 8, 8, 2), ("region_0", "region_1", "tm_0", "tm_1"))
    return jax.shard_map(
        local,
        mesh=split,
        in_specs=(
            P(TM, REGION),
            P(TM, REGION),
            P(REGION_TM, None, None, None),
            P(REGION, None),
            P(TM, None),
        ),
        out_specs=(P(TM, REGION), P(TM, REGION)),
        check_vma=False,
    )
```

```python
import jax
import jax.numpy as jnp
from jax import lax
from jax.experimental import pallas as pl
from jax.experimental.pallas import tpu as pltpu
from jax.sharding import Mesh
from jax.sharding import PartitionSpec as P


REGION = ("region_0", "region_1")
TM = ("tm_0", "tm_1")
REGION_TM = ("region_0", "region_1", "tm_0", "tm_1")
F32 = jnp.float32
BF16 = jnp.bfloat16
UNROLL = 2
VMEM = pl.BlockSpec(memory_space=pltpu.MemorySpace.VMEM)
SMEM = pl.BlockSpec(memory_space=pltpu.MemorySpace.SMEM)


def dot(a, b):
    return jnp.dot(a, b, preferred_element_type=F32)


def pack_kernel(right_ref, initial_ref, blocks_ref, slots_ref, send_ref, keep_ref, own_ref):
    hours = right_ref.shape[0]
    width, n = blocks_ref.shape[0], blocks_ref.shape[1]
    half = keep_ref.shape[0]
    for i in range(2 * half):
        lanes = slice(i * n, (i + 1) * n)
        x = initial_ref[:, lanes]
        pair = jnp.concatenate([x.astype(BF16), (right_ref[:, lanes] - x).astype(BF16)], axis=0)
        if i < half:
            send_ref[2 * hours * i : 2 * hours * (i + 1), :] = pair
        else:
            keep_ref[i - half] = pair
    base = 2 * hours * half
    extra = slots_ref.shape[0]
    send_ref[base : base + extra, :] = slots_ref[...]
    for k in range(width):
        flipped = blocks_ref[k].T
        own_ref[k * n : (k + 1) * n, :] = flipped
        send_ref[base + extra + k * n : base + extra + (k + 1) * n, :] = flipped


def temporal_kernel(core_ref, own_ref, other_ref, v_ref, w_ref, shift_ref):
    groups, part, hours = own_ref.shape
    n = v_ref.shape[2]
    core = core_ref[0]
    row = lax.broadcasted_iota(jnp.int32, (part, n), 0)
    lane = lax.broadcasted_iota(jnp.int32, (part, n), 1)
    diagonal = jnp.zeros((part, n), F32)
    for t in range(groups):
        first_row = 2 * part * t
        lanes = slice(first_row // n * n, first_row // n * n + n)
        for ref, which in ((own_ref, core), (other_ref, 1 - core)):
            at = row + (first_row % n + part * which)
            diagonal = diagonal + jnp.where(lane == at, ref[t, :, lanes].astype(F32), 0.0)
    c0 = jnp.sum(diagonal, axis=(0, 1), keepdims=True) / hours
    shift_ref[...] = jnp.broadcast_to(c0, shift_ref.shape)

    mine = own_ref[...].reshape(groups * part, hours)
    theirs = other_ref[...].reshape(groups * part, hours)

    def power(v, base):
        wide = v.shape[1]
        by_core = jnp.stack([dot(mine, v).reshape(groups, part, wide), dot(theirs, v).reshape(groups, part, wide)], axis=1)
        swapped = jnp.stack([by_core[:, 1], by_core[:, 0]], axis=1)
        full = jnp.where(core == 0, by_core, swapped).reshape(hours, wide)
        out = (full - c0 * v.astype(F32)).astype(BF16)
        w_ref[:, base : base + wide] = out
        return out

    v = v_ref[...]
    pairs = [v[:, k * 2 * part : (k + 1) * 2 * part].reshape(hours, n) for k in range(2)]
    first = power(jnp.concatenate(pairs, axis=1), 0)
    second = power(first, 2 * n)
    power(second[:, :n], 4 * n)


def spatial_kernel(
    slots_ref, g_ref, xd_ref, shift_ref, b_ref, low_ref, high_ref, gram_ref, centre_ref,
    b_buf, f_buf, z_buf, w_buf, r_buf, m_buf, t_buf, s_buf, sums, sem,
):
    rows, hours, n = r_buf.shape
    half = rows // 2
    slots = slots_ref.shape[1]

    def load(i):
        return pltpu.make_async_copy(b_ref.at[i], b_buf.at[i], sem.at[i])

    for i in range(rows):
        load(i).start()
    c0 = shift_ref[0:1, 0:1]
    for i in range(rows):
        x = xd_ref[i, 0:hours].astype(F32)
        y1 = g_ref[i, :, 0:n].astype(F32)
        y2 = g_ref[i, :, 2 * n : 3 * n].astype(F32)
        y3 = g_ref[i, :, 4 * n : 5 * n].astype(F32)
        f_buf[i, 0:hours, :] = (c0 * x + y1).astype(BF16)
        f_buf[i, hours : 2 * hours, :] = (c0 * y1 + y2).astype(BF16)
        f_buf[i, 2 * hours :, :] = (c0 * y2 + y3).astype(BF16)

    def product(source, i):
        tiles = [source[i]] + [source[slots_ref[i, k]] for k in range(slots)]
        return dot(jnp.concatenate(tiles, axis=1), b_buf[i])

    diagonal = lax.broadcasted_iota(jnp.int32, (n, n), 0) == lax.broadcasted_iota(jnp.int32, (n, n), 1)

    def stage_one(i, _):
        load(i).wait()
        block = b_buf[i, 0:n].astype(F32)
        s_buf[i] = jnp.broadcast_to(jnp.sum(jnp.where(diagonal, block, 0.0), axis=(0, 1), keepdims=True) / n, (8, n))
        out = product(f_buf, i)
        d = xd_ref[i, hours : 2 * hours].astype(F32)
        e1 = g_ref[i, :, n : 2 * n].astype(F32)
        e2 = g_ref[i, :, 3 * n : 4 * n].astype(F32)
        r0 = d - out[0:hours]
        u1 = e1 - out[hours : 2 * hours]
        u2 = e2 - out[2 * hours :]
        r_buf[i] = r0
        z1 = c0 * r0 + u1
        rest = c0 * u1 + u2
        z_buf[i, 0:hours, :] = z1.astype(BF16)
        z_buf[i, hours:, :] = rest.astype(BF16)
        m_buf[i] = z1
        t_buf[i] = rest
        return 0

    def stage_two(i, _):
        out = product(z_buf, i)
        s = s_buf[i, 0:1, :]
        first = out[0:hours] - s * z_buf[i, 0:hours].astype(F32)
        second = out[hours:] - s * z_buf[i, hours:].astype(F32)
        z1 = m_buf[i]
        w2 = s * (c0 * z1 + t_buf[i]) + c0 * first + second
        m_buf[i] = s * z1 + first
        t_buf[i] = w2
        w_buf[i] = w2.astype(BF16)
        return 0

    def add(k, value):
        sums[k] += jnp.sum(value.reshape(hours // 8, 8, n), axis=0)

    def stage_three(mu, low, i):
        s = s_buf[i, 0:1, :]
        m2 = product(w_buf, i) - s * w_buf[i].astype(F32) + s * t_buf[i]
        r0, m1 = r_buf[i], m_buf[i]
        add(0, r0 * r0)
        add(1, r0 * m1)
        add(2, m1 * m1)
        add(3, r0 * m2)
        add(4, m1 * m2)
        centred = (r0, m1 - mu * r0, m2 - mu * (2.0 * m1 - mu * r0))
        for k, value in enumerate(centred):
            if low:
                start = pl.multiple_of((k * half + i) * hours, hours)
                low_ref[pl.ds(start, hours), :] = value.astype(BF16)
            else:
                high_ref[k, i - half] = value

    sums[...] = jnp.zeros_like(sums)
    lax.fori_loop(0, rows, stage_one, 0, unroll=UNROLL)
    lax.fori_loop(0, rows, stage_two, 0, unroll=UNROLL)
    mean = jnp.sum(s_buf[:, 0:1, :], axis=0) / rows
    rounded = (c0 * mean).astype(BF16)
    mu = rounded.astype(F32)
    centre_ref[...] = jnp.broadcast_to(mu, centre_ref.shape)
    low_ref[3 * half * hours :, :] = jnp.broadcast_to(mu, (16, n)).astype(BF16)
    lax.fori_loop(0, half, lambda i, _: (stage_three(mu, True, i), 0)[1], 0, unroll=UNROLL)
    lax.fori_loop(half, rows, lambda i, _: (stage_three(mu, False, i), 0)[1], 0, unroll=UNROLL)
    gram = jnp.sum(sums[...], axis=1)
    for k in range(gram_ref.shape[0]):
        gram_ref[k] = gram


def finish_kernel(gram_ref, x_ref, low_ref, high_ref, centre_ref, solution_ref, residual_ref):
    total = jnp.sum(jnp.sum(gram_ref[...], axis=0), axis=1, keepdims=True)
    rr, rm1, m11, rm2, m12 = (total[k : k + 1, 0:1] for k in range(5))
    rq = rr + rm1
    qq = rr + 2.0 * rm1 + m11
    rs = rr + 2.0 * rm1 + rm2
    qs = rr + 3.0 * rm1 + rm2 + 2.0 * m11 + m12
    alpha = rr / rq
    norm = rr - 2.0 * alpha * rq + alpha * alpha * qq
    keep = 1.0 + norm / rr
    curvature = keep * keep * rq - alpha * keep * (rs + qq) + alpha * alpha * qs
    step = norm / curvature
    x_0 = alpha + step * (keep - alpha)
    x_1 = -step * alpha
    g_0 = 1.0 - x_0
    g_1 = -alpha - step * (keep - 2.0 * alpha)
    g_2 = step * alpha
    _, half, hours, n = high_ref.shape

    def write(mu, first, load):
        a_0, a_1 = x_0 + mu * x_1, x_1
        b_0, b_1, b_2 = g_0 + mu * (g_1 + mu * g_2), g_1 + 2.0 * mu * g_2, g_2
        for i in range(half):
            lanes = slice((first + i) * n, (first + i + 1) * n)
            r0, e1, e2 = load(0, i), load(1, i), load(2, i)
            solution_ref[:, lanes] = x_ref[:, lanes] + (a_0 * r0 + a_1 * e1)
            residual_ref[:, lanes] = b_0 * r0 + b_1 * e1 + b_2 * e2

    write(centre_ref[0:1, 0:1], half, lambda k, i: high_ref[k, i])
    base = 3 * half * hours
    write(
        low_ref[base : base + 16, :].astype(F32)[0:1, 0:1],
        0,
        lambda k, i: low_ref[(k * half + i) * hours : (k * half + i + 1) * hours, :].astype(F32),
    )


def steps(right_side, initial, blocks, neighbour_blocks, temporal_cov):
    hours, sites = right_side.shape
    n = blocks.shape[2]
    width = blocks.shape[1]
    rows = neighbour_blocks.shape[0]
    half = rows // 2
    slots = neighbour_blocks.shape[1]
    tm_count = lax.axis_size(TM)
    regions = lax.axis_size(REGION)
    all_hours = temporal_cov.shape[1]
    part = hours // 2

    local_slots = lax.rem(neighbour_blocks, rows)
    extra = jnp.pad(local_slots[:half].astype(BF16), ((0, 16 - half), (0, n - slots)))
    base = 2 * hours * half
    halves = jnp.broadcast_to(temporal_cov.reshape(1, 2, part, all_hours), (tm_count // 2, 2, part, all_hours))
    mine = lax.all_to_all(
        halves.reshape(tm_count, part, all_hours), TM, split_axis=0, concat_axis=0, tiled=True
    )
    packed, keep, own_blocks = pl.pallas_call(
        pack_kernel,
        out_shape=(
            jax.ShapeDtypeStruct((base + 16 + width * n, n), BF16),
            jax.ShapeDtypeStruct((half, 2 * hours, n), BF16),
            jax.ShapeDtypeStruct((width * n, n), BF16),
        ),
        in_specs=[VMEM] * 4,
        out_specs=(VMEM,) * 3,
        name="pack",
    )(right_side, initial, blocks[0], extra)
    shifted = lax.ppermute(packed, REGION, [((r + 1) % regions, r) for r in range(regions)])
    window_row = jnp.where(lax.axis_index(TM) < half, shifted[base + 16 :], own_blocks)
    window_blocks = lax.all_gather(window_row[None], TM, axis=0, tiled=True)
    xd = jnp.concatenate([shifted[:base].reshape(half, 2 * hours, n), keep], axis=0)
    window_slots = jnp.concatenate(
        [shifted[base : base + half, :slots].astype(jnp.int32), local_slots[half:]], axis=0
    )

    theirs = lax.ppermute(mine, TM[1], [(0, 1), (1, 0)])
    core = lax.axis_index(TM[1]).astype(jnp.int32).reshape(1)
    arrived = lax.all_to_all(xd, TM, split_axis=0, concat_axis=0, tiled=True)
    powers, shift = pl.pallas_call(
        temporal_kernel,
        out_shape=(
            jax.ShapeDtypeStruct((all_hours, 5 * n), BF16),
            jax.ShapeDtypeStruct((8, n), F32),
        ),
        in_specs=[SMEM, VMEM, VMEM, VMEM],
        out_specs=(VMEM, VMEM),
        name="temporal",
    )(core, mine, theirs, arrived)
    returned = lax.all_to_all(powers.reshape(tm_count, hours, 5 * n), TM, split_axis=0, concat_axis=0, tiled=True)

    low, high, gram, centre = pl.pallas_call(
        spatial_kernel,
        out_shape=(
            jax.ShapeDtypeStruct((3 * half * hours + 16, n), BF16),
            jax.ShapeDtypeStruct((3, half, hours, n), F32),
            jax.ShapeDtypeStruct((tm_count, 8, n), F32),
            jax.ShapeDtypeStruct((8, n), F32),
        ),
        in_specs=[SMEM, VMEM, VMEM, VMEM, pl.BlockSpec(memory_space=pl.ANY)],
        out_specs=(VMEM,) * 4,
        scratch_shapes=[
            pltpu.VMEM((rows, width * n, n), BF16),
            pltpu.VMEM((rows, 3 * hours, n), BF16),
            pltpu.VMEM((rows, 2 * hours, n), BF16),
            pltpu.VMEM((rows, hours, n), BF16),
            pltpu.VMEM((rows, hours, n), F32),
            pltpu.VMEM((rows, hours, n), F32),
            pltpu.VMEM((rows, hours, n), F32),
            pltpu.VMEM((rows, 8, n), F32),
            pltpu.VMEM((8, 8, n), F32),
            pltpu.SemaphoreType.DMA((rows,)),
        ],
        name="spatial",
    )(window_slots, returned, xd, shift, window_blocks)

    back = lax.ppermute(low, REGION, [(r, (r + 1) % regions) for r in range(regions)])
    over_tm = lax.all_to_all(gram, TM, split_axis=0, concat_axis=0, tiled=True)
    spread = jnp.broadcast_to(jnp.sum(over_tm, axis=0)[None], (regions, 8, n))
    over_region = lax.all_to_all(spread, REGION, split_axis=0, concat_axis=0, tiled=True)
    return pl.pallas_call(
        finish_kernel,
        out_shape=(
            jax.ShapeDtypeStruct((hours, sites), F32),
            jax.ShapeDtypeStruct((hours, sites), F32),
        ),
        in_specs=[VMEM] * 5,
        out_specs=(VMEM, VMEM),
        name="finish",
    )(over_region, initial, back, high, centre)


def solution(mesh):
    split = Mesh(mesh.devices.reshape(4, 8, 8, 2), ("region_0", "region_1", "tm_0", "tm_1"))
    return jax.shard_map(
        steps,
        mesh=split,
        in_specs=(
            P(TM, REGION),
            P(TM, REGION),
            P(REGION_TM, None, None, None),
            P(REGION, None),
            P(TM, None),
        ),
        out_specs=(P(TM, REGION), P(TM, REGION)),
        check_vma=False,
    )
```

```python
import jax
import jax.numpy as jnp
from jax import lax
from jax.experimental import pallas as pl
from jax.experimental.pallas import tpu as pltpu
from jax.sharding import Mesh
from jax.sharding import PartitionSpec as P


REGION = ("region_0", "region_1")
TM = ("tm_0", "tm_1")
REGION_TM = ("region_0", "region_1", "tm_0", "tm_1")
F32 = jnp.float32
BF16 = jnp.bfloat16
UNROLL = 2
VMEM = pl.BlockSpec(memory_space=pltpu.MemorySpace.VMEM)
SMEM = pl.BlockSpec(memory_space=pltpu.MemorySpace.SMEM)


def dot(a, b):
    return jnp.dot(a, b, preferred_element_type=F32)


def pack_kernel(right_ref, initial_ref, blocks_ref, slots_ref, send_ref, keep_ref, own_ref):
    hours = right_ref.shape[0]
    width, n = blocks_ref.shape[0], blocks_ref.shape[1]
    half = keep_ref.shape[0]
    for i in range(2 * half):
        lanes = slice(i * n, (i + 1) * n)
        x = initial_ref[:, lanes]
        pair = jnp.concatenate([x.astype(BF16), (right_ref[:, lanes] - x).astype(BF16)], axis=0)
        if i < half:
            send_ref[2 * hours * i : 2 * hours * (i + 1), :] = pair
        else:
            keep_ref[i - half] = pair
    send_ref[2 * hours * half :, :] = slots_ref[...]
    for k in range(width):
        own_ref[k * n : (k + 1) * n, :] = blocks_ref[k].T


def temporal_kernel(core_ref, own_ref, other_ref, v_ref, w_ref, shift_ref):
    groups, part, hours = own_ref.shape
    n = v_ref.shape[2]
    core = core_ref[0]
    row = lax.broadcasted_iota(jnp.int32, (part, n), 0)
    lane = lax.broadcasted_iota(jnp.int32, (part, n), 1)
    diagonal = jnp.zeros((part, n), F32)
    for t in range(groups):
        first_row = 2 * part * t
        lanes = slice(first_row // n * n, first_row // n * n + n)
        for ref, which in ((own_ref, core), (other_ref, 1 - core)):
            at = row + (first_row % n + part * which)
            diagonal = diagonal + jnp.where(lane == at, ref[t, :, lanes].astype(F32), 0.0)
    c0 = jnp.sum(diagonal, axis=(0, 1), keepdims=True) / hours
    shift_ref[...] = jnp.broadcast_to(c0, shift_ref.shape)

    mine = own_ref[...].reshape(groups * part, hours)
    theirs = other_ref[...].reshape(groups * part, hours)

    def power(v, base):
        wide = v.shape[1]
        by_core = jnp.stack([dot(mine, v).reshape(groups, part, wide), dot(theirs, v).reshape(groups, part, wide)], axis=1)
        swapped = jnp.stack([by_core[:, 1], by_core[:, 0]], axis=1)
        full = jnp.where(core == 0, by_core, swapped).reshape(hours, wide)
        out = (full - c0 * v.astype(F32)).astype(BF16)
        w_ref[:, base : base + wide] = out
        return out

    v = v_ref[...]
    pairs = [v[:, k * 2 * part : (k + 1) * 2 * part].reshape(hours, n) for k in range(2)]
    first = power(jnp.concatenate(pairs, axis=1), 0)
    second = power(first, 2 * n)
    power(second[:, :n], 4 * n)


def spatial_kernel(tm_ref, slots_ref, g_ref, xd_ref, shift_ref, *refs):
    parts, refs = refs[:10], refs[10:]
    low_ref, high_ref, gram_ref, centre_ref, b_buf, f_buf, z_buf, w_buf, r_buf, m_buf, t_buf, s_buf, sums, sem = refs
    rows, hours, n = r_buf.shape
    half = rows // 2
    slots = slots_ref.shape[1]
    deep = b_buf.shape[1]

    sources = [ref.at[...] for ref in parts[:8]]
    for ref in parts[8:]:
        sources += [ref.at[k * deep : (k + 1) * deep] for k in range(ref.shape[0] // deep)]
    for k in range(rows):
        pltpu.make_async_copy(sources[k], b_buf.at[k], sem.at[k]).start()
    position = tm_ref[0]

    def place(i):
        away = lax.rem(position // 2 - i // 2 + half, half)
        order = jnp.where(
            away == half // 2,
            half - 1,
            jnp.where(away < half // 2, jnp.maximum(2 * away - 1, 0), 2 * (half - away)),
        )
        return order + half * (lax.rem(i, 2) != lax.rem(position, 2)).astype(jnp.int32)

    c0 = shift_ref[0:1, 0:1]
    for i in range(rows):
        x = xd_ref[i, 0:hours].astype(F32)
        y1 = g_ref[i, :, 0:n].astype(F32)
        y2 = g_ref[i, :, 2 * n : 3 * n].astype(F32)
        y3 = g_ref[i, :, 4 * n : 5 * n].astype(F32)
        f_buf[i, 0:hours, :] = (c0 * x + y1).astype(BF16)
        f_buf[i, hours : 2 * hours, :] = (c0 * y1 + y2).astype(BF16)
        f_buf[i, 2 * hours :, :] = (c0 * y2 + y3).astype(BF16)

    def product(source, i):
        tiles = [source[i]] + [source[slots_ref[i, k]] for k in range(slots)]
        return dot(jnp.concatenate(tiles, axis=1), b_buf[place(i)])

    diagonal = lax.broadcasted_iota(jnp.int32, (n, n), 0) == lax.broadcasted_iota(jnp.int32, (n, n), 1)

    def stage_one(i, _):
        at = place(i)
        pltpu.make_async_copy(sources[0], b_buf.at[at], sem.at[at]).wait()
        block = b_buf[at, 0:n].astype(F32)
        s_buf[i] = jnp.broadcast_to(jnp.sum(jnp.where(diagonal, block, 0.0), axis=(0, 1), keepdims=True) / n, (8, n))
        out = product(f_buf, i)
        d = xd_ref[i, hours : 2 * hours].astype(F32)
        e1 = g_ref[i, :, n : 2 * n].astype(F32)
        e2 = g_ref[i, :, 3 * n : 4 * n].astype(F32)
        r0 = d - out[0:hours]
        u1 = e1 - out[hours : 2 * hours]
        u2 = e2 - out[2 * hours :]
        r_buf[i] = r0
        z1 = c0 * r0 + u1
        rest = c0 * u1 + u2
        z_buf[i, 0:hours, :] = z1.astype(BF16)
        z_buf[i, hours:, :] = rest.astype(BF16)
        m_buf[i] = z1
        t_buf[i] = rest
        return 0

    def stage_two(i, _):
        out = product(z_buf, i)
        s = s_buf[i, 0:1, :]
        first = out[0:hours] - s * z_buf[i, 0:hours].astype(F32)
        second = out[hours:] - s * z_buf[i, hours:].astype(F32)
        z1 = m_buf[i]
        w2 = s * (c0 * z1 + t_buf[i]) + c0 * first + second
        m_buf[i] = s * z1 + first
        t_buf[i] = w2
        w_buf[i] = w2.astype(BF16)
        return 0

    def add(k, value):
        sums[k] += jnp.sum(value.reshape(hours // 8, 8, n), axis=0)

    def stage_three(mu, low, i):
        s = s_buf[i, 0:1, :]
        m2 = product(w_buf, i) - s * w_buf[i].astype(F32) + s * t_buf[i]
        r0, m1 = r_buf[i], m_buf[i]
        add(0, r0 * r0)
        add(1, r0 * m1)
        add(2, m1 * m1)
        add(3, r0 * m2)
        add(4, m1 * m2)
        centred = (r0, m1 - mu * r0, m2 - mu * (2.0 * m1 - mu * r0))
        for k, value in enumerate(centred):
            if low:
                start = pl.multiple_of((k * half + i) * hours, hours)
                low_ref[pl.ds(start, hours), :] = value.astype(BF16)
            else:
                high_ref[k, i - half] = value

    sums[...] = jnp.zeros_like(sums)
    lax.fori_loop(0, rows, stage_one, 0, unroll=UNROLL)
    lax.fori_loop(0, rows, stage_two, 0, unroll=UNROLL)
    mean = jnp.sum(s_buf[:, 0:1, :], axis=0) / rows
    rounded = (c0 * mean).astype(BF16)
    mu = rounded.astype(F32)
    centre_ref[...] = jnp.broadcast_to(mu, centre_ref.shape)
    low_ref[3 * half * hours :, :] = jnp.broadcast_to(mu, (16, n)).astype(BF16)
    lax.fori_loop(0, half, lambda i, _: (stage_three(mu, True, i), 0)[1], 0, unroll=UNROLL)
    lax.fori_loop(half, rows, lambda i, _: (stage_three(mu, False, i), 0)[1], 0, unroll=UNROLL)
    gram = jnp.sum(sums[...], axis=1)
    for k in range(gram_ref.shape[0]):
        gram_ref[k] = gram


def finish_kernel(gram_ref, x_ref, low_ref, high_ref, centre_ref, solution_ref, residual_ref):
    total = jnp.sum(jnp.sum(gram_ref[...], axis=0), axis=1, keepdims=True)
    rr, rm1, m11, rm2, m12 = (total[k : k + 1, 0:1] for k in range(5))
    rq = rr + rm1
    qq = rr + 2.0 * rm1 + m11
    rs = rr + 2.0 * rm1 + rm2
    qs = rr + 3.0 * rm1 + rm2 + 2.0 * m11 + m12
    alpha = rr / rq
    norm = rr - 2.0 * alpha * rq + alpha * alpha * qq
    keep = 1.0 + norm / rr
    curvature = keep * keep * rq - alpha * keep * (rs + qq) + alpha * alpha * qs
    step = norm / curvature
    x_0 = alpha + step * (keep - alpha)
    x_1 = -step * alpha
    g_0 = 1.0 - x_0
    g_1 = -alpha - step * (keep - 2.0 * alpha)
    g_2 = step * alpha
    _, half, hours, n = high_ref.shape

    def write(mu, first, load):
        a_0, a_1 = x_0 + mu * x_1, x_1
        b_0, b_1, b_2 = g_0 + mu * (g_1 + mu * g_2), g_1 + 2.0 * mu * g_2, g_2
        for i in range(half):
            lanes = slice((first + i) * n, (first + i + 1) * n)
            r0, e1, e2 = load(0, i), load(1, i), load(2, i)
            solution_ref[:, lanes] = x_ref[:, lanes] + (a_0 * r0 + a_1 * e1)
            residual_ref[:, lanes] = b_0 * r0 + b_1 * e1 + b_2 * e2

    write(centre_ref[0:1, 0:1], half, lambda k, i: high_ref[k, i])
    base = 3 * half * hours
    write(
        low_ref[base : base + 16, :].astype(F32)[0:1, 0:1],
        0,
        lambda k, i: low_ref[(k * half + i) * hours : (k * half + i + 1) * hours, :].astype(F32),
    )


def ring(row):
    count = lax.axis_size(TM[0])
    up = [(i, (i + 1) % count) for i in range(count)]
    down = [(j, i) for i, j in up]
    found = [row]
    forward = backward = row
    for k in range(1, count // 2 + 1):
        forward = lax.ppermute(forward, TM[0], up)
        found.append(forward)
        if k < count // 2:
            backward = lax.ppermute(backward, TM[0], down)
            found.append(backward)
    return found[:5], found[5:]


def steps(right_side, initial, blocks, neighbour_blocks, temporal_cov):
    hours, sites = right_side.shape
    n = blocks.shape[2]
    width = blocks.shape[1]
    rows = neighbour_blocks.shape[0]
    half = rows // 2
    slots = neighbour_blocks.shape[1]
    tm_count = lax.axis_size(TM)
    regions = lax.axis_size(REGION)
    all_hours = temporal_cov.shape[1]
    part = hours // 2

    local_slots = lax.rem(neighbour_blocks, rows)
    extra = jnp.pad(local_slots[:half].astype(BF16), ((0, 16 - half), (0, n - slots)))
    base = 2 * hours * half
    halves = jnp.broadcast_to(temporal_cov.reshape(1, 2, part, all_hours), (tm_count // 2, 2, part, all_hours))
    mine = lax.all_to_all(
        halves.reshape(tm_count, part, all_hours), TM, split_axis=0, concat_axis=0, tiled=True
    )
    packed, keep, own_blocks = pl.pallas_call(
        pack_kernel,
        out_shape=(
            jax.ShapeDtypeStruct((base + 16, n), BF16),
            jax.ShapeDtypeStruct((half, 2 * hours, n), BF16),
            jax.ShapeDtypeStruct((width * n, n), BF16),
        ),
        in_specs=[VMEM] * 4,
        out_specs=(VMEM,) * 3,
        name="pack",
    )(right_side, initial, blocks[0], extra)
    shifted = lax.ppermute(packed, REGION, [((r + 1) % regions, r) for r in range(regions)])
    pairs = [
        (((r + (t < half)) % regions) * tm_count + t, r * tm_count + t) for r in range(regions) for t in range(tm_count)
    ]
    row = lax.ppermute(own_blocks, REGION_TM, pairs)
    near, far = ring(row)
    other_near = lax.ppermute(jnp.concatenate(near, axis=0), TM[1], [(0, 1), (1, 0)])
    other_far = lax.ppermute(jnp.concatenate(far, axis=0), TM[1], [(0, 1), (1, 0)])
    xd = jnp.concatenate([shifted[:base].reshape(half, 2 * hours, n), keep], axis=0)
    window_slots = jnp.concatenate([shifted[base : base + half, :slots].astype(jnp.int32), local_slots[half:]], axis=0)

    theirs = lax.ppermute(mine, TM[1], [(0, 1), (1, 0)])
    core = lax.axis_index(TM[1]).astype(jnp.int32).reshape(1)
    position = lax.axis_index(TM).astype(jnp.int32).reshape(1)
    arrived = lax.all_to_all(xd, TM, split_axis=0, concat_axis=0, tiled=True)
    powers, shift = pl.pallas_call(
        temporal_kernel,
        out_shape=(
            jax.ShapeDtypeStruct((all_hours, 5 * n), BF16),
            jax.ShapeDtypeStruct((8, n), F32),
        ),
        in_specs=[SMEM, VMEM, VMEM, VMEM],
        out_specs=(VMEM, VMEM),
        name="temporal",
    )(core, mine, theirs, arrived)
    returned = lax.all_to_all(
        powers.reshape(tm_count, hours, 5 * n), TM, split_axis=0, concat_axis=0, tiled=True
    )

    low, high, gram, centre = pl.pallas_call(
        spatial_kernel,
        out_shape=(
            jax.ShapeDtypeStruct((3 * half * hours + 16, n), BF16),
            jax.ShapeDtypeStruct((3, half, hours, n), F32),
            jax.ShapeDtypeStruct((tm_count, 8, n), F32),
            jax.ShapeDtypeStruct((8, n), F32),
        ),
        in_specs=[SMEM, SMEM, VMEM, VMEM, VMEM] + [pl.BlockSpec(memory_space=pl.ANY)] * 10,
        out_specs=(VMEM,) * 4,
        scratch_shapes=[
            pltpu.VMEM((rows, width * n, n), BF16),
            pltpu.VMEM((rows, 3 * hours, n), BF16),
            pltpu.VMEM((rows, 2 * hours, n), BF16),
            pltpu.VMEM((rows, hours, n), BF16),
            pltpu.VMEM((rows, hours, n), F32),
            pltpu.VMEM((rows, hours, n), F32),
            pltpu.VMEM((rows, hours, n), F32),
            pltpu.VMEM((rows, 8, n), F32),
            pltpu.VMEM((8, 8, n), F32),
            pltpu.SemaphoreType.DMA((rows,)),
        ],
        name="spatial",
    )(position, window_slots, returned, xd, shift, *near, *far, other_near, other_far)

    back = lax.ppermute(low, REGION, [(r, (r + 1) % regions) for r in range(regions)])
    over_tm = lax.all_to_all(gram, TM, split_axis=0, concat_axis=0, tiled=True)
    spread = jnp.broadcast_to(jnp.sum(over_tm, axis=0)[None], (regions, 8, n))
    over_region = lax.all_to_all(spread, REGION, split_axis=0, concat_axis=0, tiled=True)
    return pl.pallas_call(
        finish_kernel,
        out_shape=(
            jax.ShapeDtypeStruct((hours, sites), F32),
            jax.ShapeDtypeStruct((hours, sites), F32),
        ),
        in_specs=[VMEM] * 5,
        out_specs=(VMEM, VMEM),
        name="finish",
    )(over_region, initial, back, high, centre)


def solution(mesh):
    split = Mesh(mesh.devices.reshape(4, 8, 8, 2), ("region_0", "region_1", "tm_0", "tm_1"))
    return jax.shard_map(
        steps,
        mesh=split,
        in_specs=(
            P(TM, REGION),
            P(TM, REGION),
            P(REGION_TM, None, None, None),
            P(REGION, None),
            P(TM, None),
        ),
        out_specs=(P(TM, REGION), P(TM, REGION)),
        check_vma=False,
    )
```

```python
import jax
import jax.numpy as jnp
from jax import lax
from jax.experimental import pallas as pl
from jax.experimental.pallas import tpu as pltpu
from jax.sharding import Mesh
from jax.sharding import PartitionSpec as P


REGION = ("region_0", "region_1")
TM = ("tm_0", "tm_1")
REGION_TM = ("region_0", "region_1", "tm_0", "tm_1")
F32 = jnp.float32
BF16 = jnp.bfloat16
UNROLL = 2
VMEM = pl.BlockSpec(memory_space=pltpu.MemorySpace.VMEM)
SMEM = pl.BlockSpec(memory_space=pltpu.MemorySpace.SMEM)


def dot(a, b):
    return jnp.dot(a, b, preferred_element_type=F32)


def pack_kernel(right_ref, initial_ref, blocks_ref, slots_ref, send_ref, keep_ref, own_ref):
    hours = right_ref.shape[0]
    width, n = blocks_ref.shape[0], blocks_ref.shape[1]
    half = keep_ref.shape[0]
    for i in range(2 * half):
        lanes = slice(i * n, (i + 1) * n)
        x = initial_ref[:, lanes]
        pair = jnp.concatenate([x.astype(BF16), (right_ref[:, lanes] - x).astype(BF16)], axis=0)
        if i < half:
            send_ref[2 * hours * i : 2 * hours * (i + 1), :] = pair
        else:
            keep_ref[i - half] = pair
    send_ref[2 * hours * half :, :] = slots_ref[...]
    for k in range(width):
        own_ref[k * n : (k + 1) * n, :] = blocks_ref[k].T


def chip_order(position, half):
    away = [0]
    for k in range(1, half // 2 + 1):
        away += [k, half - k] if 2 * k < half else [k]
    return [lax.rem(position // 2 + half - k, half) for k in away]


def temporal_kernel(tm_ref, own_near, own_far, other_near, other_far, v_ref, w_ref, shift_ref):
    groups, hours, _ = w_ref.shape
    half, n = groups // 2, v_ref.shape[2]
    count = groups * hours
    core = lax.rem(tm_ref[0], 2)
    chips = chip_order(tm_ref[0], half)
    split = own_near.shape[0] // hours
    row = lax.broadcasted_iota(jnp.int32, (hours, n), 0)
    lane = lax.broadcasted_iota(jnp.int32, (hours, n), 1)
    diagonal = jnp.zeros((hours, n), F32)
    places = []
    for which, refs in ((core, (own_near, own_far)), (1 - core, (other_near, other_far))):
        for part, first in ((0, 0), (1, split)):
            group = []
            for k in range(refs[part].shape[0] // hours):
                chip = chips[first + k]
                tile = refs[part][k * hours : (k + 1) * hours, pl.ds(pl.multiple_of(chip * n, n), n)]
                diagonal = diagonal + jnp.where(lane == row + hours * which, tile.astype(F32), 0.0)
                group.append(2 * chip + which)
            places.append((refs[part], group))
    c0 = jnp.sum(diagonal, axis=(0, 1), keepdims=True) / count
    shift_ref[...] = jnp.broadcast_to(c0, shift_ref.shape)

    def power(whole, piece, base):
        wide = whole.shape[1]
        for ref, group in places:
            out = dot(ref[...], whole)
            for k, t in enumerate(group):
                value = out[k * hours : (k + 1) * hours] - c0 * piece(t).astype(F32)
                w_ref[t, :, base : base + wide] = value.astype(BF16)

    x = v_ref[:, 0:hours].reshape(count, n)
    d = v_ref[:, hours : 2 * hours].reshape(count, n)
    power(
        jnp.concatenate([x, d], axis=1),
        lambda t: jnp.concatenate([v_ref[t, 0:hours], v_ref[t, hours : 2 * hours]], axis=1),
        0,
    )
    power(w_ref[:, :, 0 : 2 * n].reshape(count, 2 * n), lambda t: w_ref[t, :, 0 : 2 * n], 2 * n)
    power(w_ref[:, :, 2 * n : 3 * n].reshape(count, n), lambda t: w_ref[t, :, 2 * n : 3 * n], 4 * n)


def spatial_kernel(
    slots_ref, g_ref, xd_ref, shift_ref, b_ref, low_ref, high_ref, gram_ref, centre_ref,
    b_buf, f_buf, z_buf, w_buf, r_buf, m_buf, t_buf, s_buf, sums, sem,
):
    rows, hours, n = r_buf.shape
    half = rows // 2
    slots = slots_ref.shape[1]

    def load(i):
        return pltpu.make_async_copy(b_ref.at[i], b_buf.at[i], sem.at[i])

    for i in range(rows):
        load(i).start()
    c0 = shift_ref[0:1, 0:1]
    for i in range(rows):
        x = xd_ref[i, 0:hours].astype(F32)
        y1 = g_ref[i, :, 0:n].astype(F32)
        y2 = g_ref[i, :, 2 * n : 3 * n].astype(F32)
        y3 = g_ref[i, :, 4 * n : 5 * n].astype(F32)
        f_buf[i, 0:hours, :] = (c0 * x + y1).astype(BF16)
        f_buf[i, hours : 2 * hours, :] = (c0 * y1 + y2).astype(BF16)
        f_buf[i, 2 * hours :, :] = (c0 * y2 + y3).astype(BF16)

    def product(source, i):
        tiles = [source[i]] + [source[slots_ref[i, k]] for k in range(slots)]
        return dot(jnp.concatenate(tiles, axis=1), b_buf[i])

    diagonal = lax.broadcasted_iota(jnp.int32, (n, n), 0) == lax.broadcasted_iota(jnp.int32, (n, n), 1)

    def stage_one(i, _):
        load(i).wait()
        block = b_buf[i, 0:n].astype(F32)
        s_buf[i] = jnp.broadcast_to(jnp.sum(jnp.where(diagonal, block, 0.0), axis=(0, 1), keepdims=True) / n, (8, n))
        out = product(f_buf, i)
        d = xd_ref[i, hours : 2 * hours].astype(F32)
        e1 = g_ref[i, :, n : 2 * n].astype(F32)
        e2 = g_ref[i, :, 3 * n : 4 * n].astype(F32)
        r0 = d - out[0:hours]
        u1 = e1 - out[hours : 2 * hours]
        u2 = e2 - out[2 * hours :]
        r_buf[i] = r0
        z1 = c0 * r0 + u1
        rest = c0 * u1 + u2
        z_buf[i, 0:hours, :] = z1.astype(BF16)
        z_buf[i, hours:, :] = rest.astype(BF16)
        m_buf[i] = z1
        t_buf[i] = rest
        return 0

    def stage_two(i, _):
        out = product(z_buf, i)
        s = s_buf[i, 0:1, :]
        first = out[0:hours] - s * z_buf[i, 0:hours].astype(F32)
        second = out[hours:] - s * z_buf[i, hours:].astype(F32)
        z1 = m_buf[i]
        w2 = s * (c0 * z1 + t_buf[i]) + c0 * first + second
        m_buf[i] = s * z1 + first
        t_buf[i] = w2
        w_buf[i] = w2.astype(BF16)
        return 0

    def add(k, value):
        sums[k] += jnp.sum(value.reshape(hours // 8, 8, n), axis=0)

    def stage_three(mu, low, i):
        s = s_buf[i, 0:1, :]
        m2 = product(w_buf, i) - s * w_buf[i].astype(F32) + s * t_buf[i]
        r0, m1 = r_buf[i], m_buf[i]
        add(0, r0 * r0)
        add(1, r0 * m1)
        add(2, m1 * m1)
        add(3, r0 * m2)
        add(4, m1 * m2)
        centred = (r0, m1 - mu * r0, m2 - mu * (2.0 * m1 - mu * r0))
        for k, value in enumerate(centred):
            if low:
                start = pl.multiple_of((k * half + i) * hours, hours)
                low_ref[pl.ds(start, hours), :] = value.astype(BF16)
            else:
                high_ref[k, i - half] = value

    sums[...] = jnp.zeros_like(sums)
    lax.fori_loop(0, rows, stage_one, 0, unroll=UNROLL)
    lax.fori_loop(0, rows, stage_two, 0, unroll=UNROLL)
    mean = jnp.sum(s_buf[:, 0:1, :], axis=0) / rows
    rounded = (c0 * mean).astype(BF16)
    mu = rounded.astype(F32)
    centre_ref[...] = jnp.broadcast_to(mu, centre_ref.shape)
    low_ref[3 * half * hours :, :] = jnp.broadcast_to(mu, (16, n)).astype(BF16)
    lax.fori_loop(0, half, lambda i, _: (stage_three(mu, True, i), 0)[1], 0, unroll=UNROLL)
    lax.fori_loop(half, rows, lambda i, _: (stage_three(mu, False, i), 0)[1], 0, unroll=UNROLL)
    gram = jnp.sum(sums[...], axis=1)
    for k in range(gram_ref.shape[0]):
        gram_ref[k] = gram


def finish_kernel(gram_ref, x_ref, low_ref, high_ref, centre_ref, solution_ref, residual_ref):
    total = jnp.sum(jnp.sum(gram_ref[...], axis=0), axis=1, keepdims=True)
    rr, rm1, m11, rm2, m12 = (total[k : k + 1, 0:1] for k in range(5))
    rq = rr + rm1
    qq = rr + 2.0 * rm1 + m11
    rs = rr + 2.0 * rm1 + rm2
    qs = rr + 3.0 * rm1 + rm2 + 2.0 * m11 + m12
    alpha = rr / rq
    norm = rr - 2.0 * alpha * rq + alpha * alpha * qq
    keep = 1.0 + norm / rr
    curvature = keep * keep * rq - alpha * keep * (rs + qq) + alpha * alpha * qs
    step = norm / curvature
    x_0 = alpha + step * (keep - alpha)
    x_1 = -step * alpha
    g_0 = 1.0 - x_0
    g_1 = -alpha - step * (keep - 2.0 * alpha)
    g_2 = step * alpha
    _, half, hours, n = high_ref.shape

    def write(mu, first, load):
        a_0, a_1 = x_0 + mu * x_1, x_1
        b_0, b_1, b_2 = g_0 + mu * (g_1 + mu * g_2), g_1 + 2.0 * mu * g_2, g_2
        for i in range(half):
            lanes = slice((first + i) * n, (first + i + 1) * n)
            r0, e1, e2 = load(0, i), load(1, i), load(2, i)
            solution_ref[:, lanes] = x_ref[:, lanes] + (a_0 * r0 + a_1 * e1)
            residual_ref[:, lanes] = b_0 * r0 + b_1 * e1 + b_2 * e2

    write(centre_ref[0:1, 0:1], half, lambda k, i: high_ref[k, i])
    base = 3 * half * hours
    write(
        low_ref[base : base + 16, :].astype(F32)[0:1, 0:1],
        0,
        lambda k, i: low_ref[(k * half + i) * hours : (k * half + i + 1) * hours, :].astype(F32),
    )


def ring(row):
    count = lax.axis_size(TM[0])
    up = [(i, (i + 1) % count) for i in range(count)]
    down = [(j, i) for i, j in up]
    found = [row]
    forward = backward = row
    for k in range(1, count // 2 + 1):
        forward = lax.ppermute(forward, TM[0], up)
        found.append(forward)
        if k < count // 2:
            backward = lax.ppermute(backward, TM[0], down)
            found.append(backward)
    return found[:5], found[5:]


def steps(right_side, initial, blocks, neighbour_blocks, temporal_cov):
    hours, sites = right_side.shape
    n = blocks.shape[2]
    width = blocks.shape[1]
    rows = neighbour_blocks.shape[0]
    half = rows // 2
    slots = neighbour_blocks.shape[1]
    tm_count = lax.axis_size(TM)
    regions = lax.axis_size(REGION)

    local_slots = lax.rem(neighbour_blocks, rows)
    extra = jnp.pad(local_slots[:half].astype(BF16), ((0, 16 - half), (0, n - slots)))
    base = 2 * hours * half
    swap = [(0, 1), (1, 0)]
    near, far = ring(temporal_cov)
    own_near, own_far = jnp.concatenate(near, axis=0), jnp.concatenate(far, axis=0)
    other_near = lax.ppermute(own_near, TM[1], swap)
    other_far = lax.ppermute(own_far, TM[1], swap)
    covariance = (own_near, own_far, other_near, other_far)
    packed, keep, own_blocks = pl.pallas_call(
        pack_kernel,
        out_shape=(
            jax.ShapeDtypeStruct((base + 16, n), BF16),
            jax.ShapeDtypeStruct((half, 2 * hours, n), BF16),
            jax.ShapeDtypeStruct((width * n, n), BF16),
        ),
        in_specs=[VMEM] * 4,
        out_specs=(VMEM,) * 3,
        name="pack",
    )(right_side, initial, blocks[0], extra)
    shifted = lax.ppermute(packed, REGION, [((r + 1) % regions, r) for r in range(regions)])
    pairs = [
        (((r + (t < half)) % regions) * tm_count + t, r * tm_count + t) for r in range(regions) for t in range(tm_count)
    ]
    row = lax.ppermute(own_blocks, REGION_TM, pairs)
    window_blocks = lax.all_gather(row[None], TM, axis=0, tiled=True)
    xd = jnp.concatenate([shifted[:base].reshape(half, 2 * hours, n), keep], axis=0)
    window_slots = jnp.concatenate([shifted[base : base + half, :slots].astype(jnp.int32), local_slots[half:]], axis=0)

    position = lax.axis_index(TM).astype(jnp.int32).reshape(1)
    arrived = lax.all_to_all(xd, TM, split_axis=0, concat_axis=0, tiled=True)
    powers, shift = pl.pallas_call(
        temporal_kernel,
        out_shape=(
            jax.ShapeDtypeStruct((tm_count, hours, 5 * n), BF16),
            jax.ShapeDtypeStruct((8, n), F32),
        ),
        in_specs=[SMEM] + [VMEM] * 5,
        out_specs=(VMEM, VMEM),
        name="temporal",
    )(position, *covariance, arrived)
    returned = lax.all_to_all(powers, TM, split_axis=0, concat_axis=0, tiled=True)

    low, high, gram, centre = pl.pallas_call(
        spatial_kernel,
        out_shape=(
            jax.ShapeDtypeStruct((3 * half * hours + 16, n), BF16),
            jax.ShapeDtypeStruct((3, half, hours, n), F32),
            jax.ShapeDtypeStruct((tm_count, 8, n), F32),
            jax.ShapeDtypeStruct((8, n), F32),
        ),
        in_specs=[SMEM, VMEM, VMEM, VMEM, pl.BlockSpec(memory_space=pl.ANY)],
        out_specs=(VMEM,) * 4,
        scratch_shapes=[
            pltpu.VMEM((rows, width * n, n), BF16),
            pltpu.VMEM((rows, 3 * hours, n), BF16),
            pltpu.VMEM((rows, 2 * hours, n), BF16),
            pltpu.VMEM((rows, hours, n), BF16),
            pltpu.VMEM((rows, hours, n), F32),
            pltpu.VMEM((rows, hours, n), F32),
            pltpu.VMEM((rows, hours, n), F32),
            pltpu.VMEM((rows, 8, n), F32),
            pltpu.VMEM((8, 8, n), F32),
            pltpu.SemaphoreType.DMA((rows,)),
        ],
        name="spatial",
    )(window_slots, returned, xd, shift, window_blocks)

    back = lax.ppermute(low, REGION, [(r, (r + 1) % regions) for r in range(regions)])
    over_tm = lax.all_to_all(gram, TM, split_axis=0, concat_axis=0, tiled=True)
    spread = jnp.broadcast_to(jnp.sum(over_tm, axis=0)[None], (regions, 8, n))
    over_region = lax.all_to_all(spread, REGION, split_axis=0, concat_axis=0, tiled=True)
    return pl.pallas_call(
        finish_kernel,
        out_shape=(
            jax.ShapeDtypeStruct((hours, sites), F32),
            jax.ShapeDtypeStruct((hours, sites), F32),
        ),
        in_specs=[VMEM] * 5,
        out_specs=(VMEM, VMEM),
        name="finish",
    )(over_region, initial, back, high, centre)


def solution(mesh):
    split = Mesh(mesh.devices.reshape(4, 8, 8, 2), ("region_0", "region_1", "tm_0", "tm_1"))
    return jax.shard_map(
        steps,
        mesh=split,
        in_specs=(
            P(TM, REGION),
            P(TM, REGION),
            P(REGION_TM, None, None, None),
            P(REGION, None),
            P(TM, None),
        ),
        out_specs=(P(TM, REGION), P(TM, REGION)),
        check_vma=False,
    )
```

```python
import jax
import jax.numpy as jnp
from jax import lax
from jax.experimental import pallas as pl
from jax.experimental.pallas import tpu as pltpu
from jax.sharding import Mesh
from jax.sharding import PartitionSpec as P


REGION = ("region_0", "region_1")
TM = ("tm_0", "tm_1")
REGION_TM = ("region_0", "region_1", "tm_0", "tm_1")
F32 = jnp.float32
BF16 = jnp.bfloat16
UNROLL = 2
VMEM = pl.BlockSpec(memory_space=pltpu.MemorySpace.VMEM)
SMEM = pl.BlockSpec(memory_space=pltpu.MemorySpace.SMEM)


def dot(a, b):
    return jnp.dot(a, b, preferred_element_type=F32)


def keep_in_vmem(value):
    return pltpu.with_memory_space_constraint(value, pltpu.MemorySpace.VMEM)


def pack_kernel(right_ref, initial_ref, blocks_ref, slots_ref, send_ref, keep_ref, own_ref):
    hours = right_ref.shape[0]
    width, n = blocks_ref.shape[0], blocks_ref.shape[1]
    half = keep_ref.shape[0]
    for i in range(2 * half):
        lanes = slice(i * n, (i + 1) * n)
        x = initial_ref[:, lanes]
        pair = jnp.concatenate([x.astype(BF16), (right_ref[:, lanes] - x).astype(BF16)], axis=0)
        if i < half:
            send_ref[2 * hours * i : 2 * hours * (i + 1), :] = pair
        else:
            keep_ref[i - half] = pair
    send_ref[2 * hours * half :, :] = slots_ref[...]
    for k in range(width):
        own_ref[k * n : (k + 1) * n, :] = blocks_ref[k].T


def temporal_kernel(core_ref, own_ref, other_ref, v_ref, w_ref, shift_ref):
    groups, part, hours = own_ref.shape
    n = v_ref.shape[2]
    core = core_ref[0]
    row = lax.broadcasted_iota(jnp.int32, (part, n), 0)
    lane = lax.broadcasted_iota(jnp.int32, (part, n), 1)
    diagonal = jnp.zeros((part, n), F32)
    for t in range(groups):
        first_row = 2 * part * t
        lanes = slice(first_row // n * n, first_row // n * n + n)
        for ref, which in ((own_ref, core), (other_ref, 1 - core)):
            at = row + (first_row % n + part * which)
            diagonal = diagonal + jnp.where(lane == at, ref[t, :, lanes].astype(F32), 0.0)
    c0 = jnp.sum(diagonal, axis=(0, 1), keepdims=True) / hours
    shift_ref[...] = jnp.broadcast_to(c0, shift_ref.shape)

    mine = own_ref[...].reshape(groups * part, hours)
    theirs = other_ref[...].reshape(groups * part, hours)

    def power(v, base):
        wide = v.shape[1]
        by_core = jnp.stack([dot(mine, v).reshape(groups, part, wide), dot(theirs, v).reshape(groups, part, wide)], axis=1)
        swapped = jnp.stack([by_core[:, 1], by_core[:, 0]], axis=1)
        full = jnp.where(core == 0, by_core, swapped).reshape(hours, wide)
        out = (full - c0 * v.astype(F32)).astype(BF16)
        w_ref[:, base : base + wide] = out
        return out

    v = v_ref[...]
    pairs = [v[:, k * 2 * part : (k + 1) * 2 * part].reshape(hours, n) for k in range(2)]
    first = power(jnp.concatenate(pairs, axis=1), 0)
    second = power(first, 2 * n)
    power(second[:, :n], 4 * n)


def spatial_kernel(
    slots_ref, g_ref, xd_ref, shift_ref, b_ref, low_ref, high_ref, gram_ref, centre_ref,
    b_buf, f_buf, z_buf, w_buf, r_buf, m_buf, t_buf, s_buf, sums, sem,
):
    rows, hours, n = r_buf.shape
    half = rows // 2
    slots = slots_ref.shape[1]

    def load(i):
        return pltpu.make_async_copy(b_ref.at[i], b_buf.at[i], sem.at[i])

    for i in range(rows):
        load(i).start()
    c0 = shift_ref[0:1, 0:1]
    for i in range(rows):
        x = xd_ref[i, 0:hours].astype(F32)
        y1 = g_ref[i, :, 0:n].astype(F32)
        y2 = g_ref[i, :, 2 * n : 3 * n].astype(F32)
        y3 = g_ref[i, :, 4 * n : 5 * n].astype(F32)
        f_buf[i, 0:hours, :] = (c0 * x + y1).astype(BF16)
        f_buf[i, hours : 2 * hours, :] = (c0 * y1 + y2).astype(BF16)
        f_buf[i, 2 * hours :, :] = (c0 * y2 + y3).astype(BF16)

    def product(source, i):
        tiles = [source[i]] + [source[slots_ref[i, k]] for k in range(slots)]
        return dot(jnp.concatenate(tiles, axis=1), b_buf[i])

    diagonal = lax.broadcasted_iota(jnp.int32, (n, n), 0) == lax.broadcasted_iota(jnp.int32, (n, n), 1)

    def stage_one(i, _):
        load(i).wait()
        block = b_buf[i, 0:n].astype(F32)
        s_buf[i] = jnp.broadcast_to(jnp.sum(jnp.where(diagonal, block, 0.0), axis=(0, 1), keepdims=True) / n, (8, n))
        out = product(f_buf, i)
        d = xd_ref[i, hours : 2 * hours].astype(F32)
        e1 = g_ref[i, :, n : 2 * n].astype(F32)
        e2 = g_ref[i, :, 3 * n : 4 * n].astype(F32)
        r0 = d - out[0:hours]
        u1 = e1 - out[hours : 2 * hours]
        u2 = e2 - out[2 * hours :]
        r_buf[i] = r0
        z1 = c0 * r0 + u1
        rest = c0 * u1 + u2
        z_buf[i, 0:hours, :] = z1.astype(BF16)
        z_buf[i, hours:, :] = rest.astype(BF16)
        m_buf[i] = z1
        t_buf[i] = rest
        return 0

    def stage_two(i, _):
        out = product(z_buf, i)
        s = s_buf[i, 0:1, :]
        first = out[0:hours] - s * z_buf[i, 0:hours].astype(F32)
        second = out[hours:] - s * z_buf[i, hours:].astype(F32)
        z1 = m_buf[i]
        w2 = s * (c0 * z1 + t_buf[i]) + c0 * first + second
        m_buf[i] = s * z1 + first
        t_buf[i] = w2
        w_buf[i] = w2.astype(BF16)
        return 0

    def add(k, value):
        sums[k] += jnp.sum(value.reshape(hours // 8, 8, n), axis=0)

    def stage_three(mu, low, i):
        s = s_buf[i, 0:1, :]
        m2 = product(w_buf, i) - s * w_buf[i].astype(F32) + s * t_buf[i]
        r0, m1 = r_buf[i], m_buf[i]
        add(0, r0 * r0)
        add(1, r0 * m1)
        add(2, m1 * m1)
        add(3, r0 * m2)
        add(4, m1 * m2)
        centred = (r0, m1 - mu * r0, m2 - mu * (2.0 * m1 - mu * r0))
        for k, value in enumerate(centred):
            if low:
                start = pl.multiple_of((k * half + i) * hours, hours)
                low_ref[pl.ds(start, hours), :] = value.astype(BF16)
            else:
                high_ref[k, i - half] = value

    sums[...] = jnp.zeros_like(sums)
    lax.fori_loop(0, rows, stage_one, 0, unroll=UNROLL)
    lax.fori_loop(0, rows, stage_two, 0, unroll=UNROLL)
    mean = jnp.sum(s_buf[:, 0:1, :], axis=0) / rows
    rounded = (c0 * mean).astype(BF16)
    mu = rounded.astype(F32)
    centre_ref[...] = jnp.broadcast_to(mu, centre_ref.shape)
    low_ref[3 * half * hours :, :] = jnp.broadcast_to(mu, (16, n)).astype(BF16)
    lax.fori_loop(0, half, lambda i, _: (stage_three(mu, True, i), 0)[1], 0, unroll=UNROLL)
    lax.fori_loop(half, rows, lambda i, _: (stage_three(mu, False, i), 0)[1], 0, unroll=UNROLL)
    gram = jnp.sum(sums[...], axis=1)
    for k in range(gram_ref.shape[0]):
        gram_ref[k] = gram


def finish_kernel(gram_ref, x_ref, low_ref, high_ref, centre_ref, solution_ref, residual_ref):
    total = jnp.sum(jnp.sum(gram_ref[...], axis=0), axis=1, keepdims=True)
    rr, rm1, m11, rm2, m12 = (total[k : k + 1, 0:1] for k in range(5))
    rq = rr + rm1
    qq = rr + 2.0 * rm1 + m11
    rs = rr + 2.0 * rm1 + rm2
    qs = rr + 3.0 * rm1 + rm2 + 2.0 * m11 + m12
    alpha = rr / rq
    norm = rr - 2.0 * alpha * rq + alpha * alpha * qq
    keep = 1.0 + norm / rr
    curvature = keep * keep * rq - alpha * keep * (rs + qq) + alpha * alpha * qs
    step = norm / curvature
    x_0 = alpha + step * (keep - alpha)
    x_1 = -step * alpha
    g_0 = 1.0 - x_0
    g_1 = -alpha - step * (keep - 2.0 * alpha)
    g_2 = step * alpha
    _, half, hours, n = high_ref.shape

    def write(mu, first, load):
        a_0, a_1 = x_0 + mu * x_1, x_1
        b_0, b_1, b_2 = g_0 + mu * (g_1 + mu * g_2), g_1 + 2.0 * mu * g_2, g_2
        for i in range(half):
            lanes = slice((first + i) * n, (first + i + 1) * n)
            r0, e1, e2 = load(0, i), load(1, i), load(2, i)
            solution_ref[:, lanes] = x_ref[:, lanes] + (a_0 * r0 + a_1 * e1)
            residual_ref[:, lanes] = b_0 * r0 + b_1 * e1 + b_2 * e2

    write(centre_ref[0:1, 0:1], half, lambda k, i: high_ref[k, i])
    base = 3 * half * hours
    write(
        low_ref[base : base + 16, :].astype(F32)[0:1, 0:1],
        0,
        lambda k, i: low_ref[(k * half + i) * hours : (k * half + i + 1) * hours, :].astype(F32),
    )


def steps(right_side, initial, blocks, neighbour_blocks, temporal_cov):
    hours, sites = right_side.shape
    n = blocks.shape[2]
    width = blocks.shape[1]
    rows = neighbour_blocks.shape[0]
    half = rows // 2
    slots = neighbour_blocks.shape[1]
    tm_count = lax.axis_size(TM)
    regions = lax.axis_size(REGION)
    all_hours = temporal_cov.shape[1]
    part = hours // 2

    local_slots = lax.rem(neighbour_blocks, rows)
    extra = jnp.pad(local_slots[:half].astype(BF16), ((0, 16 - half), (0, n - slots)))
    base = 2 * hours * half
    halves = jnp.broadcast_to(temporal_cov.reshape(1, 2, part, all_hours), (tm_count // 2, 2, part, all_hours))
    mine = lax.all_to_all(
        halves.reshape(tm_count, part, all_hours), TM, split_axis=0, concat_axis=0, tiled=True
    )
    packed, keep, own_blocks = pl.pallas_call(
        pack_kernel,
        out_shape=(
            jax.ShapeDtypeStruct((base + 16, n), BF16),
            jax.ShapeDtypeStruct((half, 2 * hours, n), BF16),
            jax.ShapeDtypeStruct((width * n, n), BF16),
        ),
        in_specs=[VMEM] * 4,
        out_specs=(VMEM,) * 3,
        name="pack",
    )(right_side, initial, blocks[0], extra)
    shifted = lax.ppermute(packed, REGION, [((r + 1) % regions, r) for r in range(regions)])
    pairs = [
        (((r + (t < half)) % regions) * tm_count + t, r * tm_count + t) for r in range(regions) for t in range(tm_count)
    ]
    row = lax.ppermute(own_blocks, REGION_TM, pairs)
    window_blocks = lax.all_gather(row[None], TM, axis=0, tiled=True)
    xd = jnp.concatenate([shifted[:base].reshape(half, 2 * hours, n), keep], axis=0)
    window_slots = jnp.concatenate(
        [shifted[base : base + half, :slots].astype(jnp.int32), local_slots[half:]], axis=0
    )

    theirs = lax.ppermute(mine, TM[1], [(0, 1), (1, 0)])
    core = lax.axis_index(TM[1]).astype(jnp.int32).reshape(1)
    arrived = lax.all_to_all(xd, TM, split_axis=0, concat_axis=0, tiled=True)
    powers, shift = pl.pallas_call(
        temporal_kernel,
        out_shape=(
            jax.ShapeDtypeStruct((all_hours, 5 * n), BF16),
            jax.ShapeDtypeStruct((8, n), F32),
        ),
        in_specs=[SMEM, VMEM, VMEM, VMEM],
        out_specs=(VMEM, VMEM),
        name="temporal",
    )(core, keep_in_vmem(mine), keep_in_vmem(theirs), keep_in_vmem(arrived))
    returned = lax.all_to_all(powers.reshape(tm_count, hours, 5 * n), TM, split_axis=0, concat_axis=0, tiled=True)

    low, high, gram, centre = pl.pallas_call(
        spatial_kernel,
        out_shape=(
            jax.ShapeDtypeStruct((3 * half * hours + 16, n), BF16),
            jax.ShapeDtypeStruct((3, half, hours, n), F32),
            jax.ShapeDtypeStruct((tm_count, 8, n), F32),
            jax.ShapeDtypeStruct((8, n), F32),
        ),
        in_specs=[SMEM, VMEM, VMEM, VMEM, pl.BlockSpec(memory_space=pl.ANY)],
        out_specs=(VMEM,) * 4,
        scratch_shapes=[
            pltpu.VMEM((rows, width * n, n), BF16),
            pltpu.VMEM((rows, 3 * hours, n), BF16),
            pltpu.VMEM((rows, 2 * hours, n), BF16),
            pltpu.VMEM((rows, hours, n), BF16),
            pltpu.VMEM((rows, hours, n), F32),
            pltpu.VMEM((rows, hours, n), F32),
            pltpu.VMEM((rows, hours, n), F32),
            pltpu.VMEM((rows, 8, n), F32),
            pltpu.VMEM((8, 8, n), F32),
            pltpu.SemaphoreType.DMA((rows,)),
        ],
        name="spatial",
    )(window_slots, keep_in_vmem(returned), keep_in_vmem(xd), shift, window_blocks)

    back = lax.ppermute(low, REGION, [(r, (r + 1) % regions) for r in range(regions)])
    over_tm = lax.all_to_all(gram, TM, split_axis=0, concat_axis=0, tiled=True)
    spread = jnp.broadcast_to(jnp.sum(over_tm, axis=0)[None], (regions, 8, n))
    over_region = lax.all_to_all(spread, REGION, split_axis=0, concat_axis=0, tiled=True)
    return pl.pallas_call(
        finish_kernel,
        out_shape=(
            jax.ShapeDtypeStruct((hours, sites), F32),
            jax.ShapeDtypeStruct((hours, sites), F32),
        ),
        in_specs=[VMEM] * 5,
        out_specs=(VMEM, VMEM),
        name="finish",
    )(over_region, initial, keep_in_vmem(back), high, centre)


def solution(mesh):
    split = Mesh(mesh.devices.reshape(4, 8, 8, 2), ("region_0", "region_1", "tm_0", "tm_1"))
    return jax.shard_map(
        steps,
        mesh=split,
        in_specs=(
            P(TM, REGION),
            P(TM, REGION),
            P(REGION_TM, None, None, None),
            P(REGION, None),
            P(TM, None),
        ),
        out_specs=(P(TM, REGION), P(TM, REGION)),
        check_vma=False,
    )
```

```python
import jax
import jax.numpy as jnp
from jax import lax
from jax.experimental import pallas as pl
from jax.experimental.pallas import tpu as pltpu
from jax.sharding import Mesh
from jax.sharding import PartitionSpec as P


REGION = ("region_0", "region_1")
TM = ("tm_0", "tm_1")
REGION_TM = ("region_0", "region_1", "tm_0", "tm_1")
F32 = jnp.float32
BF16 = jnp.bfloat16
UNROLL = 8
VMEM = pl.BlockSpec(memory_space=pltpu.MemorySpace.VMEM)
SMEM = pl.BlockSpec(memory_space=pltpu.MemorySpace.SMEM)


def dot(a, b):
    return jnp.dot(a, b, preferred_element_type=F32)


def keep_in_vmem(value):
    return pltpu.with_memory_space_constraint(value, pltpu.MemorySpace.VMEM)


def pack_kernel(right_ref, initial_ref, blocks_ref, send_ref, keep_ref, own_ref):
    width, n = blocks_ref.shape[0], blocks_ref.shape[1]
    half = keep_ref.shape[0]
    for i in range(2 * half):
        lanes = slice(i * n, (i + 1) * n)
        x = initial_ref[:, lanes]
        pair = jnp.concatenate([x.astype(BF16), (right_ref[:, lanes] - x).astype(BF16)], axis=0)
        if i < half:
            send_ref[i] = pair
        else:
            keep_ref[i - half] = pair
    for k in range(width):
        own_ref[k * n : (k + 1) * n, :] = blocks_ref[k].T


def spread_kernel(chip_ref, rows_ref, out_ref):
    groups, part, wide = out_ref.shape
    chips = groups // 2
    n = rows_ref.shape[1] // chips
    for k in range(wide // n):
        start = pl.multiple_of(lax.rem(chip_ref[0] + k, chips) * n, n)
        for core in range(2):
            tile = rows_ref[core * part : (core + 1) * part, pl.ds(start, n)]
            for chip in range(chips):
                out_ref[2 * chip + core, :, k * n : (k + 1) * n] = tile


def temporal_kernel(core_ref, own_ref, other_ref, v_ref, w_ref, shift_ref, c_buf):
    groups, part, wide = own_ref.shape
    chips = groups // 2
    n = v_ref.shape[2]
    hours = chips * n
    core = core_ref[0]
    for t in range(groups):
        for ref, which in ((own_ref, core), (other_ref, 1 - core)):
            rows = pl.ds(pl.multiple_of(2 * part * t + part * which, part), part)
            for k in range(wide // n):
                block = (t // 2 + k) % chips
                c_buf[rows, block * n : (block + 1) * n] = ref[t, :, k * n : (k + 1) * n]
    for i in range(chips):
        for k in range(1, chips // 2):
            j = (i + k) % chips
            c_buf[j * n : (j + 1) * n, i * n : (i + 1) * n] = c_buf[i * n : (i + 1) * n, j * n : (j + 1) * n].T
    eye = lax.broadcasted_iota(jnp.int32, (n, n), 0) == lax.broadcasted_iota(jnp.int32, (n, n), 1)
    diagonal = jnp.zeros((n, n), F32)
    for i in range(chips):
        tile = c_buf[i * n : (i + 1) * n, i * n : (i + 1) * n].astype(F32)
        diagonal = diagonal + jnp.where(eye, tile, 0.0)
    c0 = jnp.sum(diagonal, axis=(0, 1), keepdims=True) / hours
    shift_ref[...] = jnp.broadcast_to(c0, shift_ref.shape)

    def power(v, base):
        out = (dot(c_buf[...], v) - c0 * v.astype(F32)).astype(BF16)
        w_ref[:, base : base + v.shape[1]] = out
        return out

    v = v_ref[...]
    pairs = [v[:, k * 2 * part : (k + 1) * 2 * part].reshape(hours, n) for k in range(2)]
    first = power(jnp.concatenate(pairs, axis=1), 0)
    second = power(first, 2 * n)
    power(second[:, :n], 4 * n)


def spatial_kernel(
    slots_ref, g_ref, xd_ref, shift_ref, b_ref, low_ref, high_ref, gram_ref, centre_ref,
    b_buf, f_buf, z_buf, w_buf, r_buf, m_buf, t_buf, s_buf, sums, sem,
):
    rows, hours, n = r_buf.shape
    half = rows // 2
    slots = slots_ref.shape[1]

    def load(i):
        return pltpu.make_async_copy(b_ref.at[i], b_buf.at[i], sem.at[i])

    for i in range(rows):
        load(i).start()
    c0 = shift_ref[0:1, 0:1]
    for i in range(rows):
        x = xd_ref[i, 0:hours].astype(F32)
        y1 = g_ref[i, :, 0:n].astype(F32)
        y2 = g_ref[i, :, 2 * n : 3 * n].astype(F32)
        y3 = g_ref[i, :, 4 * n : 5 * n].astype(F32)
        f_buf[i, 0:hours, :] = (c0 * x + y1).astype(BF16)
        f_buf[i, hours : 2 * hours, :] = (c0 * y1 + y2).astype(BF16)
        f_buf[i, 2 * hours :, :] = (c0 * y2 + y3).astype(BF16)

    def product(source, i):
        tiles = [source[i]] + [source[slots_ref[i, k]] for k in range(slots)]
        return dot(jnp.concatenate(tiles, axis=1), b_buf[i])

    diagonal = lax.broadcasted_iota(jnp.int32, (n, n), 0) == lax.broadcasted_iota(jnp.int32, (n, n), 1)

    def stage_one(i, _):
        load(i).wait()
        block = b_buf[i, 0:n].astype(F32)
        s_buf[i] = jnp.broadcast_to(jnp.sum(jnp.where(diagonal, block, 0.0), axis=(0, 1), keepdims=True) / n, (8, n))
        out = product(f_buf, i)
        d = xd_ref[i, hours : 2 * hours].astype(F32)
        e1 = g_ref[i, :, n : 2 * n].astype(F32)
        e2 = g_ref[i, :, 3 * n : 4 * n].astype(F32)
        r0 = d - out[0:hours]
        u1 = e1 - out[hours : 2 * hours]
        u2 = e2 - out[2 * hours :]
        r_buf[i] = r0
        z1 = c0 * r0 + u1
        rest = c0 * u1 + u2
        z_buf[i, 0:hours, :] = z1.astype(BF16)
        z_buf[i, hours:, :] = rest.astype(BF16)
        m_buf[i] = z1
        t_buf[i] = rest
        return 0

    def stage_two(i, _):
        out = product(z_buf, i)
        s = s_buf[i, 0:1, :]
        first = out[0:hours] - s * z_buf[i, 0:hours].astype(F32)
        second = out[hours:] - s * z_buf[i, hours:].astype(F32)
        z1 = m_buf[i]
        w2 = s * (c0 * z1 + t_buf[i]) + c0 * first + second
        m_buf[i] = s * z1 + first
        t_buf[i] = w2
        w_buf[i] = w2.astype(BF16)
        return 0

    def add(k, value):
        sums[k] += jnp.sum(value.reshape(hours // 8, 8, n), axis=0)

    def stage_three(mu, low, i):
        s = s_buf[i, 0:1, :]
        m2 = product(w_buf, i) - s * w_buf[i].astype(F32) + s * t_buf[i]
        r0, m1 = r_buf[i], m_buf[i]
        add(0, r0 * r0)
        add(1, r0 * m1)
        add(2, m1 * m1)
        add(3, r0 * m2)
        add(4, m1 * m2)
        centred = (r0, m1 - mu * r0, m2 - mu * (2.0 * m1 - mu * r0))
        for k, value in enumerate(centred):
            if low:
                start = pl.multiple_of((k * half + i) * hours, hours)
                low_ref[pl.ds(start, hours), :] = value.astype(BF16)
            else:
                high_ref[k, i - half] = value

    sums[...] = jnp.zeros_like(sums)
    lax.fori_loop(0, rows, stage_one, 0, unroll=UNROLL)
    lax.fori_loop(0, rows, stage_two, 0, unroll=UNROLL)
    mean = jnp.sum(s_buf[:, 0:1, :], axis=0) / rows
    rounded = (c0 * mean).astype(BF16)
    mu = rounded.astype(F32)
    centre_ref[...] = jnp.broadcast_to(mu, centre_ref.shape)
    low_ref[3 * half * hours :, :] = jnp.broadcast_to(mu, (16, n)).astype(BF16)
    lax.fori_loop(0, half, lambda i, _: (stage_three(mu, True, i), 0)[1], 0, unroll=UNROLL)
    lax.fori_loop(half, rows, lambda i, _: (stage_three(mu, False, i), 0)[1], 0, unroll=UNROLL)
    gram = jnp.sum(sums[...], axis=1)
    for k in range(gram_ref.shape[0]):
        gram_ref[k] = gram


def finish_kernel(gram_ref, x_ref, low_ref, high_ref, centre_ref, solution_ref, residual_ref):
    total = jnp.sum(jnp.sum(gram_ref[...], axis=0), axis=1, keepdims=True)
    rr, rm1, m11, rm2, m12 = (total[k : k + 1, 0:1] for k in range(5))
    rq = rr + rm1
    qq = rr + 2.0 * rm1 + m11
    rs = rr + 2.0 * rm1 + rm2
    qs = rr + 3.0 * rm1 + rm2 + 2.0 * m11 + m12
    alpha = rr / rq
    norm = rr - 2.0 * alpha * rq + alpha * alpha * qq
    keep = 1.0 + norm / rr
    curvature = keep * keep * rq - alpha * keep * (rs + qq) + alpha * alpha * qs
    step = norm / curvature
    x_0 = alpha + step * (keep - alpha)
    x_1 = -step * alpha
    g_0 = 1.0 - x_0
    g_1 = -alpha - step * (keep - 2.0 * alpha)
    g_2 = step * alpha
    _, half, hours, n = high_ref.shape

    def write(mu, first, load):
        a_0, a_1 = x_0 + mu * x_1, x_1
        b_0, b_1, b_2 = g_0 + mu * (g_1 + mu * g_2), g_1 + 2.0 * mu * g_2, g_2
        for i in range(half):
            lanes = slice((first + i) * n, (first + i + 1) * n)
            r0, e1, e2 = load(0, i), load(1, i), load(2, i)
            solution_ref[:, lanes] = x_ref[:, lanes] + (a_0 * r0 + a_1 * e1)
            residual_ref[:, lanes] = b_0 * r0 + b_1 * e1 + b_2 * e2

    write(centre_ref[0:1, 0:1], half, lambda k, i: high_ref[k, i])
    base = 3 * half * hours
    write(
        low_ref[base : base + 16, :].astype(F32)[0:1, 0:1],
        0,
        lambda k, i: low_ref[(k * half + i) * hours : (k * half + i + 1) * hours, :].astype(F32),
    )


def steps(right_side, initial, blocks, neighbour_blocks, temporal_cov):
    hours, sites = right_side.shape
    n = blocks.shape[2]
    width = blocks.shape[1]
    rows = neighbour_blocks.shape[0]
    half = rows // 2
    tm_count = lax.axis_size(TM)
    regions = lax.axis_size(REGION)
    all_hours = temporal_cov.shape[1]
    part = hours // 2

    core = lax.axis_index(TM[1]).astype(jnp.int32).reshape(1)
    chip = lax.axis_index(TM[0]).astype(jnp.int32).reshape(1)
    chips = tm_count // 2
    spread_rows = pl.pallas_call(
        spread_kernel,
        out_shape=jax.ShapeDtypeStruct((tm_count, part, (chips // 2 + 1) * (all_hours // chips)), BF16),
        in_specs=[SMEM, VMEM],
        out_specs=VMEM,
        name="spread",
    )(chip, temporal_cov)
    mine = lax.all_to_all(spread_rows, TM, split_axis=0, concat_axis=0, tiled=True)
    packed, keep, own_blocks = pl.pallas_call(
        pack_kernel,
        out_shape=(
            jax.ShapeDtypeStruct((half, 2 * hours, n), BF16),
            jax.ShapeDtypeStruct((half, 2 * hours, n), BF16),
            jax.ShapeDtypeStruct((width * n, n), BF16),
        ),
        in_specs=[VMEM] * 3,
        out_specs=(VMEM,) * 3,
        name="pack",
    )(right_side, initial, blocks[0])
    from_next = [((r + 1) % regions, r) for r in range(regions)]
    shifted = lax.ppermute(packed, REGION, from_next)
    pairs = [
        (((r + (t < half)) % regions) * tm_count + t, r * tm_count + t) for r in range(regions) for t in range(tm_count)
    ]
    row = lax.ppermute(own_blocks, REGION_TM, pairs)
    window_blocks = lax.all_gather(row[None], TM, axis=0, tiled=True)
    xd = jnp.concatenate([shifted, keep], axis=0)
    local_slots = lax.rem(neighbour_blocks, rows)
    next_slots = lax.ppermute(local_slots[:half], REGION, from_next)
    window_slots = jnp.concatenate([next_slots, local_slots[half:]], axis=0)

    theirs = lax.ppermute(mine, TM[1], [(0, 1), (1, 0)])
    arrived = lax.all_to_all(xd, TM, split_axis=0, concat_axis=0, tiled=True)
    powers, shift = pl.pallas_call(
        temporal_kernel,
        out_shape=(
            jax.ShapeDtypeStruct((all_hours, 5 * n), BF16),
            jax.ShapeDtypeStruct((8, n), F32),
        ),
        in_specs=[SMEM, VMEM, VMEM, VMEM],
        out_specs=(VMEM, VMEM),
        scratch_shapes=[pltpu.VMEM((all_hours, all_hours), BF16)],
        name="temporal",
    )(core, keep_in_vmem(mine), keep_in_vmem(theirs), keep_in_vmem(arrived))
    returned = lax.all_to_all(powers.reshape(tm_count, hours, 5 * n), TM, split_axis=0, concat_axis=0, tiled=True)

    low, high, gram, centre = pl.pallas_call(
        spatial_kernel,
        out_shape=(
            jax.ShapeDtypeStruct((3 * half * hours + 16, n), BF16),
            jax.ShapeDtypeStruct((3, half, hours, n), F32),
            jax.ShapeDtypeStruct((tm_count, 8, n), F32),
            jax.ShapeDtypeStruct((8, n), F32),
        ),
        in_specs=[SMEM, VMEM, VMEM, VMEM, pl.BlockSpec(memory_space=pl.ANY)],
        out_specs=(VMEM,) * 4,
        scratch_shapes=[
            pltpu.VMEM((rows, width * n, n), BF16),
            pltpu.VMEM((rows, 3 * hours, n), BF16),
            pltpu.VMEM((rows, 2 * hours, n), BF16),
            pltpu.VMEM((rows, hours, n), BF16),
            pltpu.VMEM((rows, hours, n), F32),
            pltpu.VMEM((rows, hours, n), F32),
            pltpu.VMEM((rows, hours, n), F32),
            pltpu.VMEM((rows, 8, n), F32),
            pltpu.VMEM((8, 8, n), F32),
            pltpu.SemaphoreType.DMA((rows,)),
        ],
        name="spatial",
    )(window_slots, keep_in_vmem(returned), keep_in_vmem(xd), shift, window_blocks)

    back = lax.ppermute(low, REGION, [(r, (r + 1) % regions) for r in range(regions)])
    over_tm = lax.all_to_all(gram, TM, split_axis=0, concat_axis=0, tiled=True)
    spread = jnp.broadcast_to(jnp.sum(over_tm, axis=0)[None], (regions, 8, n))
    over_region = lax.all_to_all(spread, REGION, split_axis=0, concat_axis=0, tiled=True)
    return pl.pallas_call(
        finish_kernel,
        out_shape=(
            jax.ShapeDtypeStruct((hours, sites), F32),
            jax.ShapeDtypeStruct((hours, sites), F32),
        ),
        in_specs=[VMEM] * 5,
        out_specs=(VMEM, VMEM),
        name="finish",
    )(over_region, keep_in_vmem(initial), keep_in_vmem(back), high, centre)


def solution(mesh):
    split = Mesh(mesh.devices.reshape(4, 8, 8, 2), ("region_0", "region_1", "tm_0", "tm_1"))
    return jax.shard_map(
        steps,
        mesh=split,
        in_specs=(
            P(TM, REGION),
            P(TM, REGION),
            P(REGION_TM, None, None, None),
            P(REGION, None),
            P(TM, None),
        ),
        out_specs=(P(TM, REGION), P(TM, REGION)),
        check_vma=False,
    )
```

```python
import jax
import jax.numpy as jnp
from jax import lax
from jax.experimental import pallas as pl
from jax.experimental.pallas import tpu as pltpu
from jax.sharding import Mesh
from jax.sharding import PartitionSpec as P


REGION = ("region_0", "region_1")
TM = ("tm_0", "tm_1")
REGION_TM = ("region_0", "region_1", "tm_0", "tm_1")
F32 = jnp.float32
BF16 = jnp.bfloat16
UNROLL = 8
VMEM = pl.BlockSpec(memory_space=pltpu.MemorySpace.VMEM)
SMEM = pl.BlockSpec(memory_space=pltpu.MemorySpace.SMEM)


def dot(a, b):
    return jnp.dot(a, b, preferred_element_type=F32)


def keep_in_vmem(value):
    return pltpu.with_memory_space_constraint(value, pltpu.MemorySpace.VMEM)


def pack_kernel(right_ref, initial_ref, send_ref, field_ref):
    half, _, n = send_ref.shape
    for i in range(2 * half):
        lanes = slice(i * n, (i + 1) * n)
        x = initial_ref[:, lanes]
        pair = jnp.concatenate([x.astype(BF16), (right_ref[:, lanes] - x).astype(BF16)], axis=0)
        if i < half:
            send_ref[i] = pair
        else:
            field_ref[i] = pair


def merge_kernel(field_ref, arrived_ref, out_ref, sem):
    del field_ref
    copy = pltpu.make_async_copy(arrived_ref, out_ref.at[0 : arrived_ref.shape[0]], sem)
    copy.start()
    copy.wait()


def flip_kernel(blocks_ref, out_ref):
    n = blocks_ref.shape[1]
    for k in range(blocks_ref.shape[0]):
        out_ref[k * n : (k + 1) * n, :] = blocks_ref[k].T


def spread_kernel(chip_ref, rows_ref, out_ref):
    groups, part, wide = out_ref.shape
    chips = groups // 2
    n = rows_ref.shape[1] // chips
    for k in range(wide // n):
        start = pl.multiple_of(lax.rem(chip_ref[0] + k, chips) * n, n)
        for core in range(2):
            tile = rows_ref[core * part : (core + 1) * part, pl.ds(start, n)]
            for chip in range(chips):
                out_ref[2 * chip + core, :, k * n : (k + 1) * n] = tile


def temporal_kernel(core_ref, own_ref, other_ref, v_ref, w_ref, shift_ref, c_buf):
    groups, part, wide = own_ref.shape
    chips = groups // 2
    n = v_ref.shape[2]
    hours = chips * n
    core = core_ref[0]
    for t in range(groups):
        for ref, which in ((own_ref, core), (other_ref, 1 - core)):
            rows = pl.ds(pl.multiple_of(2 * part * t + part * which, part), part)
            for k in range(wide // n):
                block = (t // 2 + k) % chips
                c_buf[rows, block * n : (block + 1) * n] = ref[t, :, k * n : (k + 1) * n]
    for i in range(chips):
        for k in range(1, chips // 2):
            j = (i + k) % chips
            c_buf[j * n : (j + 1) * n, i * n : (i + 1) * n] = c_buf[i * n : (i + 1) * n, j * n : (j + 1) * n].T
    eye = lax.broadcasted_iota(jnp.int32, (n, n), 0) == lax.broadcasted_iota(jnp.int32, (n, n), 1)
    diagonal = jnp.zeros((n, n), F32)
    for i in range(chips):
        tile = c_buf[i * n : (i + 1) * n, i * n : (i + 1) * n].astype(F32)
        diagonal = diagonal + jnp.where(eye, tile, 0.0)
    c0 = jnp.sum(diagonal, axis=(0, 1), keepdims=True) / hours
    shift_ref[...] = jnp.broadcast_to(c0, shift_ref.shape)

    def power(v, base):
        out = (dot(c_buf[...], v) - c0 * v.astype(F32)).astype(BF16)
        w_ref[:, base : base + v.shape[1]] = out
        return out

    v = v_ref[...]
    pairs = [v[:, k * 2 * part : (k + 1) * 2 * part].reshape(hours, n) for k in range(2)]
    first = power(jnp.concatenate(pairs, axis=1), 0)
    second = power(first, 2 * n)
    power(second[:, :n], 4 * n)


def spatial_kernel(
    slots_ref, g_ref, xd_ref, shift_ref, b_ref, low_ref, high_ref, gram_ref, centre_ref,
    b_buf, f_buf, z_buf, w_buf, r_buf, m_buf, t_buf, s_buf, sums, sem,
):
    rows, hours, n = r_buf.shape
    half = rows // 2
    slots = slots_ref.shape[1]

    def load(i):
        return pltpu.make_async_copy(b_ref.at[i], b_buf.at[i], sem.at[i])

    for i in range(rows):
        load(i).start()
    c0 = shift_ref[0:1, 0:1]
    for i in range(rows):
        x = xd_ref[i, 0:hours].astype(F32)
        y1 = g_ref[i, :, 0:n].astype(F32)
        y2 = g_ref[i, :, 2 * n : 3 * n].astype(F32)
        y3 = g_ref[i, :, 4 * n : 5 * n].astype(F32)
        f_buf[i, 0:hours, :] = (c0 * x + y1).astype(BF16)
        f_buf[i, hours : 2 * hours, :] = (c0 * y1 + y2).astype(BF16)
        f_buf[i, 2 * hours :, :] = (c0 * y2 + y3).astype(BF16)

    def product(source, i):
        tiles = [source[i]] + [source[slots_ref[i, k]] for k in range(slots)]
        return dot(jnp.concatenate(tiles, axis=1), b_buf[i])

    diagonal = lax.broadcasted_iota(jnp.int32, (n, n), 0) == lax.broadcasted_iota(jnp.int32, (n, n), 1)

    def stage_one(i, _):
        load(i).wait()
        block = b_buf[i, 0:n].astype(F32)
        s_buf[i] = jnp.broadcast_to(jnp.sum(jnp.where(diagonal, block, 0.0), axis=(0, 1), keepdims=True) / n, (8, n))
        out = product(f_buf, i)
        d = xd_ref[i, hours : 2 * hours].astype(F32)
        e1 = g_ref[i, :, n : 2 * n].astype(F32)
        e2 = g_ref[i, :, 3 * n : 4 * n].astype(F32)
        r0 = d - out[0:hours]
        u1 = e1 - out[hours : 2 * hours]
        u2 = e2 - out[2 * hours :]
        r_buf[i] = r0
        z1 = c0 * r0 + u1
        rest = c0 * u1 + u2
        z_buf[i, 0:hours, :] = z1.astype(BF16)
        z_buf[i, hours:, :] = rest.astype(BF16)
        m_buf[i] = z1
        t_buf[i] = rest
        return 0

    def stage_two(i, _):
        out = product(z_buf, i)
        s = s_buf[i, 0:1, :]
        first = out[0:hours] - s * z_buf[i, 0:hours].astype(F32)
        second = out[hours:] - s * z_buf[i, hours:].astype(F32)
        z1 = m_buf[i]
        w2 = s * (c0 * z1 + t_buf[i]) + c0 * first + second
        m_buf[i] = s * z1 + first
        t_buf[i] = w2
        w_buf[i] = w2.astype(BF16)
        return 0

    def add(k, value):
        sums[k] += jnp.sum(value.reshape(hours // 8, 8, n), axis=0)

    def stage_three(mu, low, i):
        s = s_buf[i, 0:1, :]
        m2 = product(w_buf, i) - s * w_buf[i].astype(F32) + s * t_buf[i]
        r0, m1 = r_buf[i], m_buf[i]
        add(0, r0 * r0)
        add(1, r0 * m1)
        add(2, m1 * m1)
        add(3, r0 * m2)
        add(4, m1 * m2)
        centred = (r0, m1 - mu * r0, m2 - mu * (2.0 * m1 - mu * r0))
        for k, value in enumerate(centred):
            if low:
                start = pl.multiple_of((k * half + i) * hours, hours)
                low_ref[pl.ds(start, hours), :] = value.astype(BF16)
            else:
                high_ref[k, i - half] = value

    sums[...] = jnp.zeros_like(sums)
    lax.fori_loop(0, rows, stage_one, 0, unroll=UNROLL)
    lax.fori_loop(0, rows, stage_two, 0, unroll=UNROLL)
    mean = jnp.sum(s_buf[:, 0:1, :], axis=0) / rows
    rounded = (c0 * mean).astype(BF16)
    mu = rounded.astype(F32)
    centre_ref[...] = jnp.broadcast_to(mu, centre_ref.shape)
    low_ref[3 * half * hours :, :] = jnp.broadcast_to(mu, (16, n)).astype(BF16)
    lax.fori_loop(0, half, lambda i, _: (stage_three(mu, True, i), 0)[1], 0, unroll=UNROLL)
    lax.fori_loop(half, rows, lambda i, _: (stage_three(mu, False, i), 0)[1], 0, unroll=UNROLL)
    gram = jnp.sum(sums[...], axis=1)
    for k in range(gram_ref.shape[0]):
        gram_ref[k] = gram


def finish_kernel(gram_ref, x_ref, low_ref, high_ref, centre_ref, solution_ref, residual_ref):
    total = jnp.sum(jnp.sum(gram_ref[...], axis=0), axis=1, keepdims=True)
    rr, rm1, m11, rm2, m12 = (total[k : k + 1, 0:1] for k in range(5))
    rq = rr + rm1
    qq = rr + 2.0 * rm1 + m11
    rs = rr + 2.0 * rm1 + rm2
    qs = rr + 3.0 * rm1 + rm2 + 2.0 * m11 + m12
    alpha = rr / rq
    norm = rr - 2.0 * alpha * rq + alpha * alpha * qq
    keep = 1.0 + norm / rr
    curvature = keep * keep * rq - alpha * keep * (rs + qq) + alpha * alpha * qs
    step = norm / curvature
    x_0 = alpha + step * (keep - alpha)
    x_1 = -step * alpha
    g_0 = 1.0 - x_0
    g_1 = -alpha - step * (keep - 2.0 * alpha)
    g_2 = step * alpha
    _, half, hours, n = high_ref.shape

    def write(mu, first, load):
        a_0, a_1 = x_0 + mu * x_1, x_1
        b_0, b_1, b_2 = g_0 + mu * (g_1 + mu * g_2), g_1 + 2.0 * mu * g_2, g_2
        for i in range(half):
            lanes = slice((first + i) * n, (first + i + 1) * n)
            r0, e1, e2 = load(0, i), load(1, i), load(2, i)
            solution_ref[:, lanes] = x_ref[:, lanes] + (a_0 * r0 + a_1 * e1)
            residual_ref[:, lanes] = b_0 * r0 + b_1 * e1 + b_2 * e2

    write(centre_ref[0:1, 0:1], half, lambda k, i: high_ref[k, i])
    base = 3 * half * hours
    write(
        low_ref[base : base + 16, :].astype(F32)[0:1, 0:1],
        0,
        lambda k, i: low_ref[(k * half + i) * hours : (k * half + i + 1) * hours, :].astype(F32),
    )


def steps(right_side, initial, blocks, neighbour_blocks, temporal_cov):
    hours, sites = right_side.shape
    n = blocks.shape[2]
    width = blocks.shape[1]
    rows = neighbour_blocks.shape[0]
    half = rows // 2
    tm_count = lax.axis_size(TM)
    regions = lax.axis_size(REGION)
    all_hours = temporal_cov.shape[1]
    part = hours // 2

    pairs = [
        (((r + (t < half)) % regions) * tm_count + t, r * tm_count + t) for r in range(regions) for t in range(tm_count)
    ]
    row = lax.ppermute(blocks[0], REGION_TM, pairs)
    core = lax.axis_index(TM[1]).astype(jnp.int32).reshape(1)
    chip = lax.axis_index(TM[0]).astype(jnp.int32).reshape(1)
    chips = tm_count // 2
    spread_rows = pl.pallas_call(
        spread_kernel,
        out_shape=jax.ShapeDtypeStruct((tm_count, part, (chips // 2 + 1) * (all_hours // chips)), BF16),
        in_specs=[SMEM, VMEM],
        out_specs=VMEM,
        name="spread",
    )(chip, temporal_cov)
    mine = lax.all_to_all(spread_rows, TM, split_axis=0, concat_axis=0, tiled=True)
    packed, field = pl.pallas_call(
        pack_kernel,
        out_shape=(
            jax.ShapeDtypeStruct((half, 2 * hours, n), BF16),
            jax.ShapeDtypeStruct((rows, 2 * hours, n), BF16),
        ),
        in_specs=[VMEM] * 2,
        out_specs=(VMEM, VMEM),
        name="pack",
    )(right_side, initial)
    from_next = [((r + 1) % regions, r) for r in range(regions)]
    shifted = lax.ppermute(packed, REGION, from_next)
    flipped = pl.pallas_call(
        flip_kernel,
        out_shape=jax.ShapeDtypeStruct((width * n, n), BF16),
        in_specs=[VMEM],
        out_specs=VMEM,
        name="flip",
    )(keep_in_vmem(row))
    window_blocks = lax.all_gather(flipped[None], TM, axis=0, tiled=True)
    xd = pl.pallas_call(
        merge_kernel,
        out_shape=jax.ShapeDtypeStruct((rows, 2 * hours, n), BF16),
        in_specs=[pl.BlockSpec(memory_space=pl.ANY), VMEM],
        out_specs=pl.BlockSpec(memory_space=pl.ANY),
        scratch_shapes=[pltpu.SemaphoreType.DMA],
        input_output_aliases={0: 0},
        name="merge",
    )(field, keep_in_vmem(shifted))
    local_slots = lax.rem(neighbour_blocks, rows)
    next_slots = lax.ppermute(local_slots[:half], REGION, from_next)
    window_slots = jnp.concatenate([next_slots, local_slots[half:]], axis=0)

    theirs = lax.ppermute(mine, TM[1], [(0, 1), (1, 0)])
    arrived = lax.all_to_all(xd, TM, split_axis=0, concat_axis=0, tiled=True)
    powers, shift = pl.pallas_call(
        temporal_kernel,
        out_shape=(
            jax.ShapeDtypeStruct((all_hours, 5 * n), BF16),
            jax.ShapeDtypeStruct((8, n), F32),
        ),
        in_specs=[SMEM, VMEM, VMEM, VMEM],
        out_specs=(VMEM, VMEM),
        scratch_shapes=[pltpu.VMEM((all_hours, all_hours), BF16)],
        name="temporal",
    )(core, keep_in_vmem(mine), keep_in_vmem(theirs), keep_in_vmem(arrived))
    returned = lax.all_to_all(powers.reshape(tm_count, hours, 5 * n), TM, split_axis=0, concat_axis=0, tiled=True)

    low, high, gram, centre = pl.pallas_call(
        spatial_kernel,
        out_shape=(
            jax.ShapeDtypeStruct((3 * half * hours + 16, n), BF16),
            jax.ShapeDtypeStruct((3, half, hours, n), F32),
            jax.ShapeDtypeStruct((tm_count, 8, n), F32),
            jax.ShapeDtypeStruct((8, n), F32),
        ),
        in_specs=[SMEM, VMEM, VMEM, VMEM, pl.BlockSpec(memory_space=pl.ANY)],
        out_specs=(VMEM,) * 4,
        scratch_shapes=[
            pltpu.VMEM((rows, width * n, n), BF16),
            pltpu.VMEM((rows, 3 * hours, n), BF16),
            pltpu.VMEM((rows, 2 * hours, n), BF16),
            pltpu.VMEM((rows, hours, n), BF16),
            pltpu.VMEM((rows, hours, n), F32),
            pltpu.VMEM((rows, hours, n), F32),
            pltpu.VMEM((rows, hours, n), F32),
            pltpu.VMEM((rows, 8, n), F32),
            pltpu.VMEM((8, 8, n), F32),
            pltpu.SemaphoreType.DMA((rows,)),
        ],
        name="spatial",
    )(window_slots, keep_in_vmem(returned), keep_in_vmem(xd), shift, window_blocks)

    back = lax.ppermute(low, REGION, [(r, (r + 1) % regions) for r in range(regions)])
    over_tm = lax.all_to_all(gram, TM, split_axis=0, concat_axis=0, tiled=True)
    spread = jnp.broadcast_to(jnp.sum(over_tm, axis=0)[None], (regions, 8, n))
    over_region = lax.all_to_all(spread, REGION, split_axis=0, concat_axis=0, tiled=True)
    return pl.pallas_call(
        finish_kernel,
        out_shape=(
            jax.ShapeDtypeStruct((hours, sites), F32),
            jax.ShapeDtypeStruct((hours, sites), F32),
        ),
        in_specs=[VMEM] * 5,
        out_specs=(VMEM, VMEM),
        name="finish",
    )(over_region, keep_in_vmem(initial), keep_in_vmem(back), high, centre)


def solution(mesh):
    split = Mesh(mesh.devices.reshape(4, 8, 8, 2), ("region_0", "region_1", "tm_0", "tm_1"))
    return jax.shard_map(
        steps,
        mesh=split,
        in_specs=(
            P(TM, REGION),
            P(TM, REGION),
            P(REGION_TM, None, None, None),
            P(REGION, None),
            P(TM, None),
        ),
        out_specs=(P(TM, REGION), P(TM, REGION)),
        check_vma=False,
    )
```

```python
import jax
import jax.numpy as jnp
from jax import lax
from jax.experimental import pallas as pl
from jax.experimental.pallas import tpu as pltpu
from jax.sharding import Mesh
from jax.sharding import PartitionSpec as P


REGION = ("region_0", "region_1")
TM = ("tm_0", "tm_1")
REGION_TM = ("region_0", "region_1", "tm_0", "tm_1")
F32 = jnp.float32
BF16 = jnp.bfloat16
UNROLL = 8
VMEM = pl.BlockSpec(memory_space=pltpu.MemorySpace.VMEM)
SMEM = pl.BlockSpec(memory_space=pltpu.MemorySpace.SMEM)


def dot(a, b):
    return jnp.dot(a, b, preferred_element_type=F32)


def keep_in_vmem(value):
    return pltpu.with_memory_space_constraint(value, pltpu.MemorySpace.VMEM)


def pack_kernel(right_ref, initial_ref, send_ref, field_ref):
    half, _, n = send_ref.shape
    for i in range(2 * half):
        lanes = slice(i * n, (i + 1) * n)
        x = initial_ref[:, lanes]
        pair = jnp.concatenate([x.astype(BF16), (right_ref[:, lanes] - x).astype(BF16)], axis=0)
        if i < half:
            send_ref[i] = pair
        else:
            field_ref[i] = pair


def merge_kernel(field_ref, arrived_ref, out_ref, sem):
    del field_ref
    copy = pltpu.make_async_copy(arrived_ref, out_ref.at[0 : arrived_ref.shape[0]], sem)
    copy.start()
    copy.wait()


def flip_kernel(blocks_ref, out_ref):
    n = blocks_ref.shape[1]
    for k in range(blocks_ref.shape[0]):
        out_ref[k * n : (k + 1) * n, :] = blocks_ref[k].T


def spread_kernel(chip_ref, rows_ref, out_ref):
    groups, part, wide = out_ref.shape
    chips = groups // 2
    n = rows_ref.shape[1] // chips
    for k in range(wide // n):
        start = pl.multiple_of(lax.rem(chip_ref[0] + k, chips) * n, n)
        for core in range(2):
            tile = rows_ref[core * part : (core + 1) * part, pl.ds(start, n)]
            for chip in range(chips):
                out_ref[2 * chip + core, :, k * n : (k + 1) * n] = tile


def square_kernel(core_ref, own_ref, other_ref, c_buf, shift_ref):
    groups, part, wide = own_ref.shape
    chips = groups // 2
    hours = c_buf.shape[0]
    n = hours // chips
    core = core_ref[0]
    for t in range(groups):
        for ref, which in ((own_ref, core), (other_ref, 1 - core)):
            rows = pl.ds(pl.multiple_of(2 * part * t + part * which, part), part)
            for k in range(wide // n):
                block = (t // 2 + k) % chips
                c_buf[rows, block * n : (block + 1) * n] = ref[t, :, k * n : (k + 1) * n]
    for i in range(chips):
        for k in range(1, chips // 2):
            j = (i + k) % chips
            c_buf[j * n : (j + 1) * n, i * n : (i + 1) * n] = c_buf[i * n : (i + 1) * n, j * n : (j + 1) * n].T
    eye = lax.broadcasted_iota(jnp.int32, (n, n), 0) == lax.broadcasted_iota(jnp.int32, (n, n), 1)
    diagonal = jnp.zeros((n, n), F32)
    for i in range(chips):
        tile = c_buf[i * n : (i + 1) * n, i * n : (i + 1) * n].astype(F32)
        diagonal = diagonal + jnp.where(eye, tile, 0.0)
    c0 = jnp.sum(diagonal, axis=(0, 1), keepdims=True) / hours
    shift_ref[...] = jnp.broadcast_to(c0, shift_ref.shape)


def temporal_kernel(c_ref, shift_ref, v_ref, w_ref):
    _, both, n = v_ref.shape
    hours = c_ref.shape[0]
    c0 = shift_ref[0:1, 0:1]

    def power(v, base):
        out = (dot(c_ref[...], v) - c0 * v.astype(F32)).astype(BF16)
        w_ref[:, base : base + v.shape[1]] = out
        return out

    v = v_ref[...]
    pairs = [v[:, k * both // 2 : (k + 1) * both // 2].reshape(hours, n) for k in range(2)]
    first = power(jnp.concatenate(pairs, axis=1), 0)
    second = power(first, 2 * n)
    power(second[:, :n], 4 * n)


def spatial_kernel(
    slots_ref, g_ref, xd_ref, shift_ref, b_ref, low_ref, high_ref, gram_ref, centre_ref,
    b_buf, f_buf, z_buf, w_buf, r_buf, m_buf, t_buf, s_buf, sums, sem,
):
    rows, hours, n = r_buf.shape
    half = rows // 2
    slots = slots_ref.shape[1]

    def load(i):
        return pltpu.make_async_copy(b_ref.at[i], b_buf.at[i], sem.at[i])

    for i in range(rows):
        load(i).start()
    c0 = shift_ref[0:1, 0:1]
    for i in range(rows):
        x = xd_ref[i, 0:hours].astype(F32)
        y1 = g_ref[i, :, 0:n].astype(F32)
        y2 = g_ref[i, :, 2 * n : 3 * n].astype(F32)
        y3 = g_ref[i, :, 4 * n : 5 * n].astype(F32)
        f_buf[i, 0:hours, :] = (c0 * x + y1).astype(BF16)
        f_buf[i, hours : 2 * hours, :] = (c0 * y1 + y2).astype(BF16)
        f_buf[i, 2 * hours :, :] = (c0 * y2 + y3).astype(BF16)

    def product(source, i):
        tiles = [source[i]] + [source[slots_ref[i, k]] for k in range(slots)]
        return dot(jnp.concatenate(tiles, axis=1), b_buf[i])

    diagonal = lax.broadcasted_iota(jnp.int32, (n, n), 0) == lax.broadcasted_iota(jnp.int32, (n, n), 1)

    def stage_one(i, _):
        load(i).wait()
        block = b_buf[i, 0:n].astype(F32)
        s_buf[i] = jnp.broadcast_to(jnp.sum(jnp.where(diagonal, block, 0.0), axis=(0, 1), keepdims=True) / n, (8, n))
        out = product(f_buf, i)
        d = xd_ref[i, hours : 2 * hours].astype(F32)
        e1 = g_ref[i, :, n : 2 * n].astype(F32)
        e2 = g_ref[i, :, 3 * n : 4 * n].astype(F32)
        r0 = d - out[0:hours]
        u1 = e1 - out[hours : 2 * hours]
        u2 = e2 - out[2 * hours :]
        r_buf[i] = r0
        z1 = c0 * r0 + u1
        rest = c0 * u1 + u2
        z_buf[i, 0:hours, :] = z1.astype(BF16)
        z_buf[i, hours:, :] = rest.astype(BF16)
        m_buf[i] = z1
        t_buf[i] = rest
        return 0

    def stage_two(i, _):
        out = product(z_buf, i)
        s = s_buf[i, 0:1, :]
        first = out[0:hours] - s * z_buf[i, 0:hours].astype(F32)
        second = out[hours:] - s * z_buf[i, hours:].astype(F32)
        z1 = m_buf[i]
        w2 = s * (c0 * z1 + t_buf[i]) + c0 * first + second
        m_buf[i] = s * z1 + first
        t_buf[i] = w2
        w_buf[i] = w2.astype(BF16)
        return 0

    def add(k, value):
        sums[k] += jnp.sum(value.reshape(hours // 8, 8, n), axis=0)

    def stage_three(mu, low, i):
        s = s_buf[i, 0:1, :]
        m2 = product(w_buf, i) - s * w_buf[i].astype(F32) + s * t_buf[i]
        r0, m1 = r_buf[i], m_buf[i]
        add(0, r0 * r0)
        add(1, r0 * m1)
        add(2, m1 * m1)
        add(3, r0 * m2)
        add(4, m1 * m2)
        centred = (r0, m1 - mu * r0, m2 - mu * (2.0 * m1 - mu * r0))
        for k, value in enumerate(centred):
            if low:
                start = pl.multiple_of((k * half + i) * hours, hours)
                low_ref[pl.ds(start, hours), :] = value.astype(BF16)
            else:
                high_ref[k, i - half] = value

    sums[...] = jnp.zeros_like(sums)
    lax.fori_loop(0, rows, stage_one, 0, unroll=UNROLL)
    lax.fori_loop(0, rows, stage_two, 0, unroll=UNROLL)
    mean = jnp.sum(s_buf[:, 0:1, :], axis=0) / rows
    rounded = (c0 * mean).astype(BF16)
    mu = rounded.astype(F32)
    centre_ref[...] = jnp.broadcast_to(mu, centre_ref.shape)
    low_ref[3 * half * hours :, :] = jnp.broadcast_to(mu, (16, n)).astype(BF16)
    lax.fori_loop(0, half, lambda i, _: (stage_three(mu, True, i), 0)[1], 0, unroll=UNROLL)
    lax.fori_loop(half, rows, lambda i, _: (stage_three(mu, False, i), 0)[1], 0, unroll=UNROLL)
    gram = jnp.sum(sums[...], axis=1)
    for k in range(gram_ref.shape[0]):
        gram_ref[k] = gram


def finish_kernel(gram_ref, x_ref, low_ref, high_ref, centre_ref, solution_ref, residual_ref):
    total = jnp.sum(jnp.sum(gram_ref[...], axis=0), axis=1, keepdims=True)
    rr, rm1, m11, rm2, m12 = (total[k : k + 1, 0:1] for k in range(5))
    rq = rr + rm1
    qq = rr + 2.0 * rm1 + m11
    rs = rr + 2.0 * rm1 + rm2
    qs = rr + 3.0 * rm1 + rm2 + 2.0 * m11 + m12
    alpha = rr / rq
    norm = rr - 2.0 * alpha * rq + alpha * alpha * qq
    keep = 1.0 + norm / rr
    curvature = keep * keep * rq - alpha * keep * (rs + qq) + alpha * alpha * qs
    step = norm / curvature
    x_0 = alpha + step * (keep - alpha)
    x_1 = -step * alpha
    g_0 = 1.0 - x_0
    g_1 = -alpha - step * (keep - 2.0 * alpha)
    g_2 = step * alpha
    _, half, hours, n = high_ref.shape

    def write(mu, first, load):
        a_0, a_1 = x_0 + mu * x_1, x_1
        b_0, b_1, b_2 = g_0 + mu * (g_1 + mu * g_2), g_1 + 2.0 * mu * g_2, g_2
        for i in range(half):
            lanes = slice((first + i) * n, (first + i + 1) * n)
            r0, e1, e2 = load(0, i), load(1, i), load(2, i)
            solution_ref[:, lanes] = x_ref[:, lanes] + (a_0 * r0 + a_1 * e1)
            residual_ref[:, lanes] = b_0 * r0 + b_1 * e1 + b_2 * e2

    write(centre_ref[0:1, 0:1], half, lambda k, i: high_ref[k, i])
    base = 3 * half * hours
    write(
        low_ref[base : base + 16, :].astype(F32)[0:1, 0:1],
        0,
        lambda k, i: low_ref[(k * half + i) * hours : (k * half + i + 1) * hours, :].astype(F32),
    )


def steps(right_side, initial, blocks, neighbour_blocks, temporal_cov):
    hours, sites = right_side.shape
    n = blocks.shape[2]
    width = blocks.shape[1]
    rows = neighbour_blocks.shape[0]
    half = rows // 2
    tm_count = lax.axis_size(TM)
    regions = lax.axis_size(REGION)
    all_hours = temporal_cov.shape[1]
    part = hours // 2

    pairs = [
        (((r + (t < half)) % regions) * tm_count + t, r * tm_count + t) for r in range(regions) for t in range(tm_count)
    ]
    row = lax.ppermute(blocks[0], REGION_TM, pairs)
    core = lax.axis_index(TM[1]).astype(jnp.int32).reshape(1)
    chip = lax.axis_index(TM[0]).astype(jnp.int32).reshape(1)
    chips = tm_count // 2
    spread_rows = pl.pallas_call(
        spread_kernel,
        out_shape=jax.ShapeDtypeStruct((tm_count, part, (chips // 2 + 1) * (all_hours // chips)), BF16),
        in_specs=[SMEM, VMEM],
        out_specs=VMEM,
        compiler_params=pltpu.CompilerParams(vmem_limit_bytes=8 * 2**20),
        name="spread",
    )(chip, temporal_cov)
    mine = lax.all_to_all(spread_rows, TM, split_axis=0, concat_axis=0, tiled=True)
    packed, field = pl.pallas_call(
        pack_kernel,
        out_shape=(
            jax.ShapeDtypeStruct((half, 2 * hours, n), BF16),
            jax.ShapeDtypeStruct((rows, 2 * hours, n), BF16),
        ),
        in_specs=[VMEM] * 2,
        out_specs=(VMEM, VMEM),
        compiler_params=pltpu.CompilerParams(vmem_limit_bytes=8 * 2**20),
        name="pack",
    )(right_side, initial)
    from_next = [((r + 1) % regions, r) for r in range(regions)]
    shifted = lax.ppermute(packed, REGION, from_next)
    flipped = pl.pallas_call(
        flip_kernel,
        out_shape=jax.ShapeDtypeStruct((width * n, n), BF16),
        in_specs=[VMEM],
        out_specs=VMEM,
        compiler_params=pltpu.CompilerParams(vmem_limit_bytes=8 * 2**20),
        name="flip",
    )(keep_in_vmem(row))
    window_blocks = lax.all_gather(flipped[None], TM, axis=0, tiled=True)
    xd = pl.pallas_call(
        merge_kernel,
        out_shape=jax.ShapeDtypeStruct((rows, 2 * hours, n), BF16),
        in_specs=[pl.BlockSpec(memory_space=pl.ANY), VMEM],
        out_specs=pl.BlockSpec(memory_space=pl.ANY),
        scratch_shapes=[pltpu.SemaphoreType.DMA],
        input_output_aliases={0: 0},
        compiler_params=pltpu.CompilerParams(vmem_limit_bytes=8 * 2**20),
        name="merge",
    )(field, keep_in_vmem(shifted))
    local_slots = lax.rem(neighbour_blocks, rows)
    next_slots = lax.ppermute(local_slots[:half], REGION, from_next)
    window_slots = jnp.concatenate([next_slots, local_slots[half:]], axis=0)

    theirs = lax.ppermute(mine, TM[1], [(0, 1), (1, 0)])
    arrived = lax.all_to_all(xd, TM, split_axis=0, concat_axis=0, tiled=True)
    covariance, shift = pl.pallas_call(
        square_kernel,
        out_shape=(
            jax.ShapeDtypeStruct((all_hours, all_hours), BF16),
            jax.ShapeDtypeStruct((8, n), F32),
        ),
        in_specs=[SMEM, VMEM, VMEM],
        out_specs=(VMEM, VMEM),
        compiler_params=pltpu.CompilerParams(vmem_limit_bytes=8 * 2**20),
        name="square",
    )(core, keep_in_vmem(mine), keep_in_vmem(theirs))
    powers = pl.pallas_call(
        temporal_kernel,
        out_shape=jax.ShapeDtypeStruct((all_hours, 5 * n), BF16),
        in_specs=[VMEM] * 3,
        out_specs=VMEM,
        name="temporal",
    )(covariance, shift, keep_in_vmem(arrived))
    returned = lax.all_to_all(powers.reshape(tm_count, hours, 5 * n), TM, split_axis=0, concat_axis=0, tiled=True)

    low, high, gram, centre = pl.pallas_call(
        spatial_kernel,
        out_shape=(
            jax.ShapeDtypeStruct((3 * half * hours + 16, n), BF16),
            jax.ShapeDtypeStruct((3, half, hours, n), F32),
            jax.ShapeDtypeStruct((tm_count, 8, n), F32),
            jax.ShapeDtypeStruct((8, n), F32),
        ),
        in_specs=[SMEM, VMEM, VMEM, VMEM, pl.BlockSpec(memory_space=pltpu.MemorySpace.HBM)],
        out_specs=(VMEM,) * 4,
        scratch_shapes=[
            pltpu.VMEM((rows, width * n, n), BF16),
            pltpu.VMEM((rows, 3 * hours, n), BF16),
            pltpu.VMEM((rows, 2 * hours, n), BF16),
            pltpu.VMEM((rows, hours, n), BF16),
            pltpu.VMEM((rows, hours, n), F32),
            pltpu.VMEM((rows, hours, n), F32),
            pltpu.VMEM((rows, hours, n), F32),
            pltpu.VMEM((rows, 8, n), F32),
            pltpu.VMEM((8, 8, n), F32),
            pltpu.SemaphoreType.DMA((rows,)),
        ],
        name="spatial",
    )(window_slots, keep_in_vmem(returned), keep_in_vmem(xd), shift, window_blocks)

    back = lax.ppermute(low, REGION, [(r, (r + 1) % regions) for r in range(regions)])
    over_tm = lax.all_to_all(gram, TM, split_axis=0, concat_axis=0, tiled=True)
    spread = jnp.broadcast_to(jnp.sum(over_tm, axis=0)[None], (regions, 8, n))
    over_region = lax.all_to_all(spread, REGION, split_axis=0, concat_axis=0, tiled=True)
    return pl.pallas_call(
        finish_kernel,
        out_shape=(
            jax.ShapeDtypeStruct((hours, sites), F32),
            jax.ShapeDtypeStruct((hours, sites), F32),
        ),
        in_specs=[VMEM] * 5,
        out_specs=(VMEM, VMEM),
        name="finish",
    )(over_region, keep_in_vmem(initial), keep_in_vmem(back), high, centre)


def solution(mesh):
    split = Mesh(mesh.devices.reshape(4, 8, 8, 2), ("region_0", "region_1", "tm_0", "tm_1"))
    return jax.shard_map(
        steps,
        mesh=split,
        in_specs=(
            P(TM, REGION),
            P(TM, REGION),
            P(REGION_TM, None, None, None),
            P(REGION, None),
            P(TM, None),
        ),
        out_specs=(P(TM, REGION), P(TM, REGION)),
        check_vma=False,
    )
```

```python
import jax
import jax.numpy as jnp
from jax import lax
from jax.experimental import pallas as pl
from jax.experimental.pallas import tpu as pltpu
from jax.sharding import Mesh
from jax.sharding import PartitionSpec as P


REGION = ("region_0", "region_1")
TM = ("tm_0", "tm_1")
REGION_TM = ("region_0", "region_1", "tm_0", "tm_1")
F32 = jnp.float32
BF16 = jnp.bfloat16
UNROLL = 8
VMEM = pl.BlockSpec(memory_space=pltpu.MemorySpace.VMEM)
SMEM = pl.BlockSpec(memory_space=pltpu.MemorySpace.SMEM)


def dot(a, b):
    return jnp.dot(a, b, preferred_element_type=F32)


def keep_in_vmem(value):
    return pltpu.with_memory_space_constraint(value, pltpu.MemorySpace.VMEM)


def pack_kernel(right_ref, initial_ref, send_ref, field_ref):
    half, _, n = send_ref.shape
    for i in range(2 * half):
        lanes = slice(i * n, (i + 1) * n)
        x = initial_ref[:, lanes]
        pair = jnp.concatenate([x.astype(BF16), (right_ref[:, lanes] - x).astype(BF16)], axis=0)
        if i < half:
            send_ref[i] = pair
        else:
            field_ref[i] = pair


def merge_kernel(field_ref, arrived_ref, out_ref, sem):
    del field_ref
    copy = pltpu.make_async_copy(arrived_ref, out_ref.at[0 : arrived_ref.shape[0]], sem)
    copy.start()
    copy.wait()


def flip_kernel(blocks_ref, out_ref):
    n = blocks_ref.shape[1]
    for k in range(blocks_ref.shape[0]):
        out_ref[k * n : (k + 1) * n, :] = blocks_ref[k].T


def spread_kernel(chip_ref, rows_ref, out_ref):
    groups, part, wide = out_ref.shape
    chips = groups // 2
    n = rows_ref.shape[1] // chips
    for k in range(wide // n):
        start = pl.multiple_of(lax.rem(chip_ref[0] + k, chips) * n, n)
        for core in range(2):
            tile = rows_ref[core * part : (core + 1) * part, pl.ds(start, n)]
            for chip in range(chips):
                out_ref[2 * chip + core, :, k * n : (k + 1) * n] = tile


def temporal_kernel(core_ref, own_ref, other_ref, v_ref, w_ref, shift_ref, c_buf):
    groups, part, wide = own_ref.shape
    chips = groups // 2
    n = v_ref.shape[2]
    hours = chips * n
    core = core_ref[0]
    for t in range(groups):
        for ref, which in ((own_ref, core), (other_ref, 1 - core)):
            rows = pl.ds(pl.multiple_of(2 * part * t + part * which, part), part)
            for k in range(wide // n):
                block = (t // 2 + k) % chips
                c_buf[rows, block * n : (block + 1) * n] = ref[t, :, k * n : (k + 1) * n]
    for i in range(chips):
        for k in range(1, chips // 2):
            j = (i + k) % chips
            c_buf[j * n : (j + 1) * n, i * n : (i + 1) * n] = c_buf[i * n : (i + 1) * n, j * n : (j + 1) * n].T
    eye = lax.broadcasted_iota(jnp.int32, (n, n), 0) == lax.broadcasted_iota(jnp.int32, (n, n), 1)
    diagonal = jnp.zeros((n, n), F32)
    for i in range(chips):
        tile = c_buf[i * n : (i + 1) * n, i * n : (i + 1) * n].astype(F32)
        diagonal = diagonal + jnp.where(eye, tile, 0.0)
    c0 = jnp.sum(diagonal, axis=(0, 1), keepdims=True) / hours
    shift_ref[...] = jnp.broadcast_to(c0, shift_ref.shape)

    def power(v, base):
        out = (dot(c_buf[...], v) - c0 * v.astype(F32)).astype(BF16)
        w_ref[:, base : base + v.shape[1]] = out
        return out

    v = v_ref[...]
    pairs = [v[:, k * 2 * part : (k + 1) * 2 * part].reshape(hours, n) for k in range(2)]
    first = power(jnp.concatenate(pairs, axis=1), 0)
    second = power(first, 2 * n)
    power(second[:, :n], 4 * n)


def spatial_kernel(
    slots_ref, g_ref, xd_ref, shift_ref, b_ref, low_ref, high_ref, gram_ref, centre_ref,
    b_buf, f_buf, z_buf, w_buf, r_buf, m_buf, t_buf, s_buf, sums, sem,
):
    rows, hours, n = r_buf.shape
    half = rows // 2
    slots = slots_ref.shape[1]

    def load(i):
        return pltpu.make_async_copy(b_ref.at[i], b_buf.at[i], sem.at[i])

    for i in range(rows):
        load(i).start()
    c0 = shift_ref[0:1, 0:1]
    for i in range(rows):
        x = xd_ref[i, 0:hours].astype(F32)
        y1 = g_ref[i, :, 0:n].astype(F32)
        y2 = g_ref[i, :, 2 * n : 3 * n].astype(F32)
        y3 = g_ref[i, :, 4 * n : 5 * n].astype(F32)
        f_buf[i, 0:hours, :] = (c0 * x + y1).astype(BF16)
        f_buf[i, hours : 2 * hours, :] = (c0 * y1 + y2).astype(BF16)
        f_buf[i, 2 * hours :, :] = (c0 * y2 + y3).astype(BF16)

    def product(source, i):
        tiles = [source[i]] + [source[slots_ref[i, k]] for k in range(slots)]
        return dot(jnp.concatenate(tiles, axis=1), b_buf[i])

    diagonal = lax.broadcasted_iota(jnp.int32, (n, n), 0) == lax.broadcasted_iota(jnp.int32, (n, n), 1)

    def stage_one(i, _):
        load(i).wait()
        block = b_buf[i, 0:n].astype(F32)
        s_buf[i] = jnp.broadcast_to(jnp.sum(jnp.where(diagonal, block, 0.0), axis=(0, 1), keepdims=True) / n, (8, n))
        out = product(f_buf, i)
        d = xd_ref[i, hours : 2 * hours].astype(F32)
        e1 = g_ref[i, :, n : 2 * n].astype(F32)
        e2 = g_ref[i, :, 3 * n : 4 * n].astype(F32)
        r0 = d - out[0:hours]
        u1 = e1 - out[hours : 2 * hours]
        u2 = e2 - out[2 * hours :]
        r_buf[i] = r0
        z1 = c0 * r0 + u1
        rest = c0 * u1 + u2
        z_buf[i, 0:hours, :] = z1.astype(BF16)
        z_buf[i, hours:, :] = rest.astype(BF16)
        m_buf[i] = z1
        t_buf[i] = rest
        return 0

    def stage_two(i, _):
        out = product(z_buf, i)
        s = s_buf[i, 0:1, :]
        first = out[0:hours] - s * z_buf[i, 0:hours].astype(F32)
        second = out[hours:] - s * z_buf[i, hours:].astype(F32)
        z1 = m_buf[i]
        w2 = s * (c0 * z1 + t_buf[i]) + c0 * first + second
        m_buf[i] = s * z1 + first
        t_buf[i] = w2
        w_buf[i] = w2.astype(BF16)
        return 0

    def add(k, value):
        sums[k] += jnp.sum(value.reshape(hours // 8, 8, n), axis=0)

    def stage_three(mu, low, i):
        s = s_buf[i, 0:1, :]
        m2 = product(w_buf, i) - s * w_buf[i].astype(F32) + s * t_buf[i]
        r0, m1 = r_buf[i], m_buf[i]
        add(0, r0 * r0)
        add(1, r0 * m1)
        add(2, m1 * m1)
        add(3, r0 * m2)
        add(4, m1 * m2)
        centred = (r0, m1 - mu * r0, m2 - mu * (2.0 * m1 - mu * r0))
        for k, value in enumerate(centred):
            if low:
                start = pl.multiple_of((k * half + i) * hours, hours)
                low_ref[pl.ds(start, hours), :] = value.astype(BF16)
            else:
                high_ref[k, i - half] = value

    sums[...] = jnp.zeros_like(sums)
    lax.fori_loop(0, rows, stage_one, 0, unroll=UNROLL)
    lax.fori_loop(0, rows, stage_two, 0, unroll=UNROLL)
    mean = jnp.sum(s_buf[:, 0:1, :], axis=0) / rows
    rounded = (c0 * mean).astype(BF16)
    mu = rounded.astype(F32)
    centre_ref[...] = jnp.broadcast_to(mu, centre_ref.shape)
    low_ref[3 * half * hours :, :] = jnp.broadcast_to(mu, (16, n)).astype(BF16)
    lax.fori_loop(0, half, lambda i, _: (stage_three(mu, True, i), 0)[1], 0, unroll=UNROLL)
    lax.fori_loop(half, rows, lambda i, _: (stage_three(mu, False, i), 0)[1], 0, unroll=UNROLL)
    gram = jnp.sum(sums[...], axis=1)
    for k in range(gram_ref.shape[0]):
        gram_ref[k] = gram


def finish_kernel(gram_ref, x_ref, low_ref, high_ref, centre_ref, solution_ref, residual_ref):
    total = jnp.sum(jnp.sum(gram_ref[...], axis=0), axis=1, keepdims=True)
    rr, rm1, m11, rm2, m12 = (total[k : k + 1, 0:1] for k in range(5))
    rq = rr + rm1
    qq = rr + 2.0 * rm1 + m11
    rs = rr + 2.0 * rm1 + rm2
    qs = rr + 3.0 * rm1 + rm2 + 2.0 * m11 + m12
    alpha = rr / rq
    norm = rr - 2.0 * alpha * rq + alpha * alpha * qq
    keep = 1.0 + norm / rr
    curvature = keep * keep * rq - alpha * keep * (rs + qq) + alpha * alpha * qs
    step = norm / curvature
    x_0 = alpha + step * (keep - alpha)
    x_1 = -step * alpha
    g_0 = 1.0 - x_0
    g_1 = -alpha - step * (keep - 2.0 * alpha)
    g_2 = step * alpha
    _, half, hours, n = high_ref.shape

    def write(mu, first, load):
        a_0, a_1 = x_0 + mu * x_1, x_1
        b_0, b_1, b_2 = g_0 + mu * (g_1 + mu * g_2), g_1 + 2.0 * mu * g_2, g_2
        for i in range(half):
            lanes = slice((first + i) * n, (first + i + 1) * n)
            r0, e1, e2 = load(0, i), load(1, i), load(2, i)
            solution_ref[:, lanes] = x_ref[:, lanes] + (a_0 * r0 + a_1 * e1)
            residual_ref[:, lanes] = b_0 * r0 + b_1 * e1 + b_2 * e2

    write(centre_ref[0:1, 0:1], half, lambda k, i: high_ref[k, i])
    base = 3 * half * hours
    write(
        low_ref[base : base + 16, :].astype(F32)[0:1, 0:1],
        0,
        lambda k, i: low_ref[(k * half + i) * hours : (k * half + i + 1) * hours, :].astype(F32),
    )


def steps(right_side, initial, blocks, neighbour_blocks, temporal_cov):
    hours, sites = right_side.shape
    n = blocks.shape[2]
    width = blocks.shape[1]
    rows = neighbour_blocks.shape[0]
    half = rows // 2
    tm_count = lax.axis_size(TM)
    regions = lax.axis_size(REGION)
    all_hours = temporal_cov.shape[1]
    part = hours // 2

    pairs = [
        (((r + (t < half)) % regions) * tm_count + t, r * tm_count + t) for r in range(regions) for t in range(tm_count)
    ]
    row = lax.ppermute(blocks[0], REGION_TM, pairs)
    core = lax.axis_index(TM[1]).astype(jnp.int32).reshape(1)
    chip = lax.axis_index(TM[0]).astype(jnp.int32).reshape(1)
    chips = tm_count // 2
    spread_rows = pl.pallas_call(
        spread_kernel,
        out_shape=jax.ShapeDtypeStruct((tm_count, part, (chips // 2 + 1) * (all_hours // chips)), BF16),
        in_specs=[SMEM, VMEM],
        out_specs=VMEM,
        compiler_params=pltpu.CompilerParams(vmem_limit_bytes=8 * 2**20),
        name="spread",
    )(chip, temporal_cov)
    mine = lax.all_to_all(spread_rows, TM, split_axis=0, concat_axis=0, tiled=True)
    packed, field = pl.pallas_call(
        pack_kernel,
        out_shape=(
            jax.ShapeDtypeStruct((half, 2 * hours, n), BF16),
            jax.ShapeDtypeStruct((rows, 2 * hours, n), BF16),
        ),
        in_specs=[VMEM] * 2,
        out_specs=(VMEM, VMEM),
        compiler_params=pltpu.CompilerParams(vmem_limit_bytes=8 * 2**20),
        name="pack",
    )(right_side, initial)
    from_next = [((r + 1) % regions, r) for r in range(regions)]
    shifted = lax.ppermute(packed, REGION, from_next)
    flipped = pl.pallas_call(
        flip_kernel,
        out_shape=jax.ShapeDtypeStruct((width * n, n), BF16),
        in_specs=[VMEM],
        out_specs=VMEM,
        compiler_params=pltpu.CompilerParams(vmem_limit_bytes=8 * 2**20),
        name="flip",
    )(keep_in_vmem(row))
    window_blocks = lax.all_gather(flipped[None], TM, axis=0, tiled=True)
    xd = pl.pallas_call(
        merge_kernel,
        out_shape=jax.ShapeDtypeStruct((rows, 2 * hours, n), BF16),
        in_specs=[pl.BlockSpec(memory_space=pl.ANY), VMEM],
        out_specs=pl.BlockSpec(memory_space=pl.ANY),
        scratch_shapes=[pltpu.SemaphoreType.DMA],
        input_output_aliases={0: 0},
        compiler_params=pltpu.CompilerParams(vmem_limit_bytes=8 * 2**20),
        name="merge",
    )(field, keep_in_vmem(shifted))
    local_slots = lax.rem(neighbour_blocks, rows)
    next_slots = lax.ppermute(local_slots[:half], REGION, from_next)
    window_slots = jnp.concatenate([next_slots, local_slots[half:]], axis=0)

    theirs = lax.ppermute(mine, TM[1], [(0, 1), (1, 0)])
    arrived = lax.all_to_all(xd, TM, split_axis=0, concat_axis=0, tiled=True)
    powers, shift = pl.pallas_call(
        temporal_kernel,
        out_shape=(
            jax.ShapeDtypeStruct((all_hours, 5 * n), BF16),
            jax.ShapeDtypeStruct((8, n), F32),
        ),
        in_specs=[SMEM, VMEM, VMEM, VMEM],
        out_specs=(VMEM, VMEM),
        scratch_shapes=[pltpu.VMEM((all_hours, all_hours), BF16)],
        name="temporal",
    )(core, keep_in_vmem(mine), keep_in_vmem(theirs), keep_in_vmem(arrived))
    returned = lax.all_to_all(powers.reshape(tm_count, hours, 5 * n), TM, split_axis=0, concat_axis=0, tiled=True)

    low, high, gram, centre = pl.pallas_call(
        spatial_kernel,
        out_shape=(
            jax.ShapeDtypeStruct((3 * half * hours + 16, n), BF16),
            jax.ShapeDtypeStruct((3, half, hours, n), F32),
            jax.ShapeDtypeStruct((tm_count, 8, n), F32),
            jax.ShapeDtypeStruct((8, n), F32),
        ),
        in_specs=[SMEM, VMEM, VMEM, VMEM, pl.BlockSpec(memory_space=pltpu.MemorySpace.HBM)],
        out_specs=(VMEM,) * 4,
        scratch_shapes=[
            pltpu.VMEM((rows, width * n, n), BF16),
            pltpu.VMEM((rows, 3 * hours, n), BF16),
            pltpu.VMEM((rows, 2 * hours, n), BF16),
            pltpu.VMEM((rows, hours, n), BF16),
            pltpu.VMEM((rows, hours, n), F32),
            pltpu.VMEM((rows, hours, n), F32),
            pltpu.VMEM((rows, hours, n), F32),
            pltpu.VMEM((rows, 8, n), F32),
            pltpu.VMEM((8, 8, n), F32),
            pltpu.SemaphoreType.DMA((rows,)),
        ],
        name="spatial",
    )(window_slots, keep_in_vmem(returned), keep_in_vmem(xd), shift, window_blocks)

    back = lax.ppermute(low, REGION, [(r, (r + 1) % regions) for r in range(regions)])
    over_tm = lax.all_to_all(gram, TM, split_axis=0, concat_axis=0, tiled=True)
    spread = jnp.broadcast_to(jnp.sum(over_tm, axis=0)[None], (regions, 8, n))
    over_region = lax.all_to_all(spread, REGION, split_axis=0, concat_axis=0, tiled=True)
    return pl.pallas_call(
        finish_kernel,
        out_shape=(
            jax.ShapeDtypeStruct((hours, sites), F32),
            jax.ShapeDtypeStruct((hours, sites), F32),
        ),
        in_specs=[VMEM] * 5,
        out_specs=(VMEM, VMEM),
        name="finish",
    )(over_region, keep_in_vmem(initial), keep_in_vmem(back), high, centre)


def solution(mesh):
    split = Mesh(mesh.devices.reshape(4, 8, 8, 2), ("region_0", "region_1", "tm_0", "tm_1"))
    return jax.shard_map(
        steps,
        mesh=split,
        in_specs=(
            P(TM, REGION),
            P(TM, REGION),
            P(REGION_TM, None, None, None),
            P(REGION, None),
            P(TM, None),
        ),
        out_specs=(P(TM, REGION), P(TM, REGION)),
        check_vma=False,
    )
```
